128 devices in a mesh: grp: 4 (over y), slab: 32 (over x, z, core).
Axes of the slice: x: 4, y: 4, z: 4, core: 2. Of those that a mesh axis runs over, the one named last changes fastest.
Arguments:
- state: float32 [4, 2, 256, 128, 256], P(None, None, 'grp', 'slab'), may hold values from -5.6 to 5.6
- kz_group: int32 [256], replicated, may hold values from 0 to 7, as said below
- cutoffs: int32 [3], replicated, may hold values from 28 to 32
- damping: float32 [8], replicated, may hold values from 0.005 to 0.5
- power: float32 [8], replicated, may hold values from 0.2 to 4
Outputs:
- new_state: float32 [4, 2, 256, 128, 256], P(None, None, 'grp', 'slab')
The draws below stay inside these ranges and needn't reach their ends.
Inputs may be any that keep to these rules, and one draw needn't show every extreme that they name: `kz_group`: each of the 8 groups holds exactly 32 indices.
All inputs are finite; a program needn't handle non-finite values.
Results may differ from the reference program's by a relative error of at most 0.00005.
Values sent between devices are 32-bit elements; how exact they have to be, the bound alone decides.
No kernel may reach another device: no remote copies, remote signals or barrier semaphores. Data moves between devices by JAX's collectives and lax.ppermute only.
A program may use at most 128 MiB of HBM per device.

```python
import math
import jax
import jax.numpy as jnp
from jax import lax

NX = 256
NY = 256
NZ = 256
GROUPS = 8
KX = 128
GMODES = 32


def draw_state(key, part):
    noise = jnp.clip(jax.random.normal(key, (4, 2, NZ, KX, NY), jnp.float32), -4.0, 4.0)
    rate = 0.7
    mixing = 0.6
    decay = jnp.exp(-rate * jnp.arange(KX, dtype=jnp.float32) / KX)[None, None, None, :, None]
    noise = noise * decay
    buoyant = mixing * noise[2] + 0.8 * noise[3]
    return jnp.concatenate([noise[:3], buoyant[None]], axis=0)


def draw_kz_group(key, part):
    ordering = jax.random.permutation(key, NZ)
    return (ordering // (NZ // GROUPS)).astype(jnp.int32)


def setup_inputs(seed: int = 0) -> dict:
    seeds = jax.random.split(jax.random.key(seed), 6)
    return {
        "state": draw_state(jax.random.fold_in(seeds[5], 71), 0),
        "kz_group": draw_kz_group(jax.random.fold_in(seeds[5], 71), 0),
        "cutoffs": jax.random.randint(seeds[2], (3,), 28, 33).astype(jnp.int32),
        "damping": jnp.clip(jnp.exp(jax.random.uniform(seeds[3], (GROUPS,), jnp.float32, math.log(0.005), math.log(0.5))), 0.005, 0.5),
        "power": jnp.clip(jnp.exp(jax.random.uniform(seeds[4], (GROUPS,), jnp.float32, math.log(0.2), math.log(4.0))), 0.2, 4.0),
    }


TIME_STEP = 0.25
CORIOLIS = 1.0
BRUNT_SQUARED = 2.0
EPSILON = 1e-06

def signed(index, length):
    return jnp.where(index < length // 2, index, index - length)

def to_grid(field, slot_mode, weights):
    padded = jnp.zeros((NZ, NX, NY), field.dtype)
    padded = padded.at[slot_mode, :KX, :].set(field * weights[None, :, None])
    return jnp.real(jnp.fft.ifftn(padded)) * math.sqrt(NX * NY * NZ)

def to_spectral(values, slot_mode):
    full = jnp.fft.fftn(values) / math.sqrt(NX * NY * NZ)
    return full[slot_mode][:, :KX, :]

def squared(entries):
    return jnp.real(entries) ** 2 + jnp.imag(entries) ** 2

def reference(state, kz_group, cutoffs, damping, power):
    float_type = state.dtype
    slot_mode = jnp.argsort(kz_group, stable=True).astype(jnp.int32)
    mode_z = signed(slot_mode, NZ)
    mode_x = jnp.arange(KX, dtype=jnp.int32)
    mode_y = signed(jnp.arange(NY, dtype=jnp.int32), NY)
    wave_z = (2.0 * math.pi / NZ * mode_z.astype(float_type))[:, None, None]
    wave_x = (2.0 * math.pi / NX * mode_x.astype(float_type))[None, :, None]
    wave_y = (2.0 * math.pi / NY * mode_y.astype(float_type))[None, None, :]
    spectra = state[:, 0] + 1j * state[:, 1]
    flow_x, flow_y, flow_z, buoyant = (spectra[0], spectra[1], spectra[2], spectra[3])
    swirl_x = 1j * (wave_y * flow_z - wave_z * flow_y)
    swirl_y = 1j * (wave_z * flow_x - wave_x * flow_z)
    swirl_z = 1j * (wave_x * flow_y - wave_y * flow_x)
    weights = jnp.where(mode_x == 0, 1.0, 2.0).astype(float_type)
    grids = [to_grid(field, slot_mode, weights) for field in (flow_x, flow_y, flow_z, buoyant, swirl_x, swirl_y, swirl_z)]
    grid_u, grid_v, grid_w, grid_b, grid_ox, grid_oy, grid_oz = grids
    products = [grid_v * grid_oz - grid_w * grid_oy, grid_w * grid_ox - grid_u * grid_oz, grid_u * grid_oy - grid_v * grid_ox, grid_u * grid_b, grid_v * grid_b, grid_w * grid_b]
    hats = [to_spectral(product, slot_mode) for product in products]
    kept = ((96 * jnp.abs(mode_z) <= cutoffs[2] * NZ)[:, None, None] & (96 * mode_x <= cutoffs[0] * NX)[None, :, None] & (96 * jnp.abs(mode_y) <= cutoffs[1] * NY)[None, None, :]).astype(float_type)
    moment_x, moment_y, moment_z = (kept * hats[0], kept * hats[1], kept * hats[2])
    source_b = -1j * kept * (wave_x * hats[3] + wave_y * hats[4] + wave_z * hats[5])
    cell_flux = jnp.real(flow_z) * jnp.real(buoyant) + jnp.imag(flow_z) * jnp.imag(buoyant)
    cell_energy = 0.5 * (squared(flow_x) + squared(flow_y) + squared(flow_z) + squared(buoyant) / BRUNT_SQUARED)
    modes_total = GMODES * KX * NY
    flux_mean = lax.optimization_barrier(jnp.sum(cell_flux.reshape(GROUPS, -1), axis=1)) / modes_total
    energy_mean = lax.optimization_barrier(jnp.sum(cell_energy.reshape(GROUPS, -1), axis=1)) / modes_total
    forcing = (power - flux_mean) / (2.0 * (energy_mean + EPSILON))
    forcing_slot = jnp.repeat(forcing, GMODES)[:, None, None]
    damping_slot = jnp.repeat(damping, GMODES)[:, None, None]
    right_x = flow_x + TIME_STEP * (moment_x + forcing_slot * flow_x)
    right_y = flow_y + TIME_STEP * (moment_y + forcing_slot * flow_y)
    right_z = flow_z + TIME_STEP * (moment_z + forcing_slot * flow_z)
    right_b = buoyant + TIME_STEP * source_b
    wave_sq = wave_x * wave_x + wave_y * wave_y + wave_z * wave_z
    implicit = 1.0 + TIME_STEP * damping_slot * wave_sq
    rotation = TIME_STEP * CORIOLIS
    first_den = implicit * implicit + rotation * rotation
    second_den = implicit * implicit + TIME_STEP * TIME_STEP * BRUNT_SQUARED
    new_x = (implicit * right_x + rotation * right_y) / first_den
    new_y = (implicit * right_y - rotation * right_x) / first_den
    new_z = (implicit * right_z + TIME_STEP * right_b) / second_den
    new_b = (implicit * right_b - TIME_STEP * BRUNT_SQUARED * right_z) / second_den
    inverse_sq = 1.0 / (wave_sq + (wave_sq == 0).astype(float_type))
    inner = (wave_x * new_x + wave_y * new_y + wave_z * new_z) * inverse_sq
    new_x = new_x - wave_x * inner
    new_y = new_y - wave_y * inner
    new_z = new_z - wave_z * inner
    return jnp.stack([jnp.stack([jnp.real(updated), jnp.imag(updated)]) for updated in (new_x, new_y, new_z, new_b)]).astype(float_type)
```

```python
import functools
import math

import jax
import jax.numpy as jnp
import numpy as np
from jax import lax
from jax.experimental import pallas as pl
from jax.experimental.pallas import tpu as pltpu
from jax.sharding import Mesh
from jax.sharding import PartitionSpec as P

N = 256
GROUPS = 8
KX = 128
GMODES = 32
KEPT_COLS = 88
SLAB = ("slab_0", "slab_1", "slab_2")
ALL = ("grp",) + SLAB

TWO_PI = 6.283185307179586
WAVE = TWO_PI / N
TIME_STEP = 0.25
CORIOLIS = 1.0
BRUNT_SQUARED = 2.0
EPSILON = 1e-06
SCALE = 1.0 / 4096.0
FIELDS_OUT = 6
FIELDS_BACK = 5
ROWS_OUT = 8 * FIELDS_OUT
ROWS_BACK = 8 * FIELDS_BACK

F32 = jnp.float32
BF16 = jnp.bfloat16


def halves(table):
    high = table.astype(np.float32).astype(jnp.bfloat16)
    low = (table - high.astype(np.float64)).astype(np.float32).astype(jnp.bfloat16)
    return jnp.asarray(high), jnp.asarray(low)


def angle(rows, cols):
    return 2.0 * np.pi / N * (np.outer(rows, cols) % N).astype(np.float64)


def signed(index):
    return np.where(index < N // 2, index, index - N)


def tables():
    points = np.arange(N)
    theta = angle(points, points)
    cosine, sine = np.cos(theta), np.sin(theta)
    wave = (WAVE * signed(points))[None, :]
    y_inverse = np.concatenate([cosine, sine, wave * cosine, wave * sine], axis=0)
    z_table = np.concatenate([cosine, sine], axis=1)
    weight = np.where(np.arange(KX) == 0, 1.0, 2.0) * SCALE
    x_inverse = np.concatenate([cosine[:, :KX] * weight, -sine[:, :KX] * weight], axis=1)
    x_forward = np.concatenate([cosine[:KEPT_COLS], -sine[:KEPT_COLS]], axis=0) * SCALE
    y_forward = np.concatenate([cosine, sine], axis=1)
    return [halves(t) for t in (y_inverse, z_table, x_inverse, x_forward, y_forward)]


def split(value):
    high = value.astype(BF16)
    low = (value - high.astype(F32)).astype(BF16)
    return high, low


def product(left, right, dims):
    def one(a, b):
        return lax.dot_general(a, b, (dims, ((), ())), preferred_element_type=F32)

    return one(left[0], right[0]) + (one(left[0], right[1]) + one(left[1], right[0]))


def slot_rows(group_row, slots):
    member = (lax.broadcasted_iota(jnp.int32, (GROUPS, N), 0) == group_row).astype(F32)
    earlier = (
        lax.broadcasted_iota(jnp.int32, (N, N), 0) < lax.broadcasted_iota(jnp.int32, (N, N), 1)
    ).astype(F32)
    count = jnp.dot(member.astype(BF16), earlier.astype(BF16), preferred_element_type=F32)
    first = (GMODES * lax.broadcasted_iota(jnp.int32, (GROUPS, N), 0)).astype(F32)
    place = jnp.sum(member * (first + count), axis=0, keepdims=True).astype(jnp.int32)
    return slots == place


def signed_row(shape):
    index = lax.broadcasted_iota(jnp.int32, shape, len(shape) - 1)
    return jnp.where(index < N // 2, index, index - N)


def send_kernel(state, w_high, w_low, sent, sums):
    sign = jnp.where(lax.broadcasted_iota(jnp.int32, (N, 128), 1) < 64, -1.0, 1.0).astype(F32)
    flux = jnp.zeros((128, N), F32)
    energy = jnp.zeros((128, N), F32)
    for x in range(4):
        flow_x, flow_y, flow_z, buoyant = (state[f * 4 + x] for f in range(4))
        flux = flux + flow_z * buoyant
        energy = energy + 0.5 * (
            flow_x * flow_x
            + flow_y * flow_y
            + flow_z * flow_z
            + buoyant * buoyant * (1.0 / BRUNT_SQUARED)
        )
    group = (lax.broadcasted_iota(jnp.int32, (128, N), 0) // GMODES) % 2
    parts = []
    for value in (flux, energy):
        for which in range(2):
            parts.append(jnp.sum(jnp.where(group == which, value, 0.0)))
    line = lax.broadcasted_iota(jnp.int32, (8, 128), 0)
    total = jnp.zeros((8, 128), F32)
    for k, part in enumerate(parts):
        total = jnp.where(line == k, part, total)
    sums[...] = total

    def put(slot, x, value):
        for low in range(2):
            start = slot * 8 + low * 4 + x
            sent[pl.ds(start, 128, stride=ROWS_OUT), :] = value[low * 128 : (low + 1) * 128]

    for f in range(4):
        derived = {0: 4, 2: 5}.get(f)
        rows = 1024 if derived else 512
        for pair in range(2):
            first = f * 4 + pair * 2
            piece = state[first : first + 2].reshape(256, N)
            made = product((w_high[:rows], w_low[:rows]), split(piece), ((1,), (1,)))
            for k in range(2):
                x = pair * 2 + k
                cos_part = made[0:256, k * 128 : (k + 1) * 128]
                sin_part = made[256:512, k * 128 : (k + 1) * 128]
                put(f, x, cos_part + sign * pltpu.roll(sin_part, 64, 1))
                if derived:
                    cos_part = made[512:768, k * 128 : (k + 1) * 128]
                    sin_part = made[768:1024, k * 128 : (k + 1) * 128]
                    put(derived, x, sign * pltpu.roll(cos_part, 64, 1) - sin_part)


def grid_kernel(
    came,
    groups,
    zt_high,
    zt_low,
    xi_high,
    xi_low,
    xf_high,
    xf_low,
    sent,
    wz_high,
    wz_low,
    rows_z,
    planes,
    lines,
):
    index = lax.broadcasted_iota(jnp.int32, (512, N), 0)
    picked = slot_rows(groups[0:1, :], (index // 128) * 64 + index % 64).astype(BF16)
    is_real = (lax.broadcasted_iota(jnp.int32, (512, 512), 0) % 128) < 64
    for table, out in ((zt_high, wz_high), (zt_low, wz_low)):
        moved = jnp.dot(picked, table[...], preferred_element_type=F32)
        turned = jnp.concatenate([-moved[:, N:], moved[:, :N]], axis=1)
        out[...] = jnp.where(is_real, moved, turned).astype(BF16)
    kz = lax.dot_general(
        signed_row((8, N)).astype(F32).astype(BF16),
        picked,
        (((1,), (1,)), ((), ())),
        preferred_element_type=F32,
    )
    kz = kz[0:1, :] * WAVE
    lane = lax.broadcasted_iota(jnp.int32, (1, 512), 1)
    kz_turn = jnp.where(lane % 128 < 64, kz, -kz)
    turn = jnp.where(lane % 128 < 64, 1.0, -1.0).astype(F32)
    kx = (lax.broadcasted_iota(jnp.int32, (256, 1), 0) % 128).astype(F32) * WAVE

    upper = lax.broadcasted_iota(jnp.int32, (16, 8, 128), 1) < 4

    def field(f):
        pieces = []
        for g in range(4):
            tiles = came[g * 32 : (g + 1) * 32, f * 8 : (f + 1) * 8, :].reshape(16, 2, 8, 128)
            even, odd = tiles[:, 0], tiles[:, 1]
            first = jnp.where(upper, even, pltpu.roll(odd, 4, 1))
            second = jnp.where(upper, pltpu.roll(even, 4, 1), odd)
            pieces.append(
                jnp.concatenate([first.reshape(128, 128), second.reshape(128, 128)], axis=0)
            )
        return jnp.concatenate(pieces, axis=1)

    def turned(value):
        return jnp.concatenate(
            [pltpu.roll(value[:, g * 128 : (g + 1) * 128], 64, 1) for g in range(4)], axis=1
        )

    weights = (wz_high[...], wz_low[...])

    def vertical(value, slot):
        made = product(split(value), weights, ((1,), (0,)))
        for plane in range(2):
            part = made[plane * 128 : (plane + 1) * 128]
            rows_z[slot, 0:128, plane * N : (plane + 1) * N] = part[:, :N]
            rows_z[slot, 128:256, plane * N : (plane + 1) * N] = part[:, N:]

    flow_x = field(0)
    turned_x = turned(flow_x)
    vertical(flow_x, 0)
    flow_z = field(2)
    turned_z = turned(flow_z)
    vertical(flow_z, 2)
    vertical(kx * (turn * turned_z) - kz_turn * turned_x, 5)
    flow_y = field(1)
    turned_y = turned(flow_y)
    vertical(flow_y, 1)
    vertical(field(5) + kz_turn * turned_y, 4)
    vertical(-(kx * (turn * turned_y)) - field(4), 6)
    vertical(field(3), 3)

    x_inverse = (xi_high[...], xi_low[...])
    for slot in range(7):
        planes[slot] = product(x_inverse, split(rows_z[slot]), ((1,), (0,)))

    x_forward = (xf_high[...], xf_low[...])

    def horizontal(value, slot):
        made = product(x_forward, split(value), ((1,), (0,)))
        for plane in range(2):
            low, high = plane * KEPT_COLS, (plane + 1) * KEPT_COLS
            lines[slot, low:high, 0:N] = made[0:KEPT_COLS, plane * N : (plane + 1) * N]
            lines[slot, low:high, N:] = made[KEPT_COLS:, plane * N : (plane + 1) * N]

    u, v, w, b, ox, oy, oz = range(7)
    horizontal(planes[v] * planes[oz] - planes[w] * planes[oy], 0)
    horizontal(planes[w] * planes[ox] - planes[u] * planes[oz], 1)
    horizontal(planes[u] * planes[oy] - planes[v] * planes[ox], 2)
    horizontal(planes[u] * planes[b], 3)
    horizontal(planes[v] * planes[b], 4)
    horizontal(planes[w] * planes[b], 5)

    row = lax.broadcasted_iota(jnp.int32, (2 * KEPT_COLS, 1), 0)
    kx_kept = jnp.where(row < KEPT_COLS, row, row - KEPT_COLS).astype(F32) * WAVE
    upper_kept = lax.broadcasted_iota(jnp.int32, (11, 8, 128), 1) < 4

    def slots(value):
        return product(split(value), weights, ((1,), (1,)))

    def put(value, f):
        for g in range(4):
            part = value[:, g * 128 : (g + 1) * 128]
            first = part[:KEPT_COLS].reshape(11, 8, 128)
            second = part[KEPT_COLS:].reshape(11, 8, 128)
            even = jnp.where(upper_kept, first, pltpu.roll(second, 4, 1))
            odd = jnp.where(upper_kept, pltpu.roll(first, 4, 1), second)
            for j in range(11):
                sent[g * 32 + 2 * j, f * 8 : (f + 1) * 8, :] = even[j]
                sent[g * 32 + 2 * j + 1, f * 8 : (f + 1) * 8, :] = odd[j]

    for k in range(3):
        put(slots(lines[k]), k)
    put(slots(kx_kept * lines[3]) + kz * slots(lines[5]), 3)
    put(slots(lines[4]), 4)
    for g in range(4):
        sent[g * 32 + 22 : (g + 1) * 32] = jnp.zeros((10, ROWS_BACK, 128), F32)


def update_kernel(
    integers, reals, came, state, groups, yf_high, yf_low, made_state
):
    grp, slab = integers[0], integers[1]
    cut_x, cut_y, cut_z = integers[2], integers[3], integers[4]
    index = lax.broadcasted_iota(jnp.int32, (64, N), 0)
    picked = slot_rows(groups[0:1, :], index + grp * 64)
    mode_z = jnp.sum(jnp.where(picked, signed_row((64, N)), 0), axis=1, keepdims=True)
    mode_y = signed_row((1, N))
    slot = lax.broadcasted_iota(jnp.int32, (64, 1), 0)
    forcing = jnp.where(slot < GMODES, reals[0], reals[1])
    damping = jnp.where(slot < GMODES, reals[2], reals[3])
    wave_z = mode_z.astype(F32) * WAVE
    wave_y = mode_y.astype(F32) * WAVE
    kept_zy = (96 * jnp.abs(mode_z) <= cut_z * N) & (96 * jnp.abs(mode_y) <= cut_y * N)
    table = (yf_high[...], yf_low[...])
    wave_zy = wave_y * wave_y + wave_z * wave_z
    grown = 1.0 + TIME_STEP * forcing
    rotation = TIME_STEP * CORIOLIS
    for x in range(4):
        mode_x = slab * 4 + x
        wave_x = mode_x.astype(F32) * WAVE
        kept = kept_zy & (96 * mode_x <= cut_x * N)

        def spectral(f):
            pieces = [
                came[pl.ds(f * 8 + low * 4 + x, 128, stride=ROWS_BACK), :].T for low in range(2)
            ]
            got = product(split(jnp.concatenate(pieces, axis=1)), table, ((1,), (0,)))
            real = got[0:64, :N] + got[64:128, N:]
            imag = got[64:128, :N] - got[0:64, N:]
            return real, imag

        moments = [spectral(f) for f in range(3)]
        partial_b = spectral(3)
        flux_y = spectral(4)
        source = [partial_b[k] + wave_y * flux_y[k] for k in range(2)]
        sources = (source[1], -source[0])
        wave_sq = wave_x * wave_x + wave_zy
        implicit = 1.0 + TIME_STEP * damping * wave_sq
        square = implicit * implicit
        first = 1.0 / (square + rotation * rotation)
        second = 1.0 / (square + TIME_STEP * TIME_STEP * BRUNT_SQUARED)
        inverse_sq = 1.0 / jnp.where(wave_sq == 0, 1.0, wave_sq)
        for k in range(2):
            rows = slice(k * 64, (k + 1) * 64)
            flows = [state[f * 4 + x, rows, :] for f in range(4)]
            right = [
                flows[f] * grown + jnp.where(kept, TIME_STEP * moments[f][k], 0.0)
                for f in range(3)
            ]
            right_b = flows[3] + jnp.where(kept, TIME_STEP * sources[k], 0.0)
            new_x = (implicit * right[0] + rotation * right[1]) * first
            new_y = (implicit * right[1] - rotation * right[0]) * first
            new_z = (implicit * right[2] + TIME_STEP * right_b) * second
            new_b = (implicit * right_b - TIME_STEP * BRUNT_SQUARED * right[2]) * second
            inner = (wave_x * new_x + wave_y * new_y + wave_z * new_z) * inverse_sq
            made_state[x, rows, :] = new_x - wave_x * inner
            made_state[4 + x, rows, :] = new_y - wave_y * inner
            made_state[8 + x, rows, :] = new_z - wave_z * inner
            made_state[12 + x, rows, :] = new_b


VM = pl.BlockSpec(memory_space=pltpu.VMEM)
SM = pl.BlockSpec(memory_space=pltpu.SMEM)


def shards(state, kz_group, cutoffs, damping, power):
    grp = lax.axis_index("grp")
    slab = lax.axis_index(SLAB)
    y_inverse, z_table, x_inverse, x_forward, y_forward = tables()
    groups = jnp.broadcast_to(kz_group[None, :], (8, N))
    rows = state.transpose(0, 3, 1, 2, 4).reshape(16, 128, N)

    sent, sums = pl.pallas_call(
        send_kernel,
        out_shape=(
            jax.ShapeDtypeStruct((128 * ROWS_OUT, 128), F32),
            jax.ShapeDtypeStruct((8, 128), F32),
        ),
        in_specs=[VM] * 3,
        out_specs=(VM, VM),
        name="send",
    )(rows, *y_inverse)
    came = lax.all_to_all(sent.reshape(128, ROWS_OUT, 128), ALL, 0, 0, tiled=True)
    for axis in SLAB:
        sums = lax.psum(sums, axis)

    back = pl.pallas_call(
        grid_kernel,
        out_shape=jax.ShapeDtypeStruct((128, ROWS_BACK, 128), F32),
        in_specs=[VM] * 8,
        out_specs=VM,
        scratch_shapes=[
            pltpu.VMEM((512, 512), BF16),
            pltpu.VMEM((512, 512), BF16),
            pltpu.VMEM((7, 256, 512), F32),
            pltpu.VMEM((7, 256, 512), F32),
            pltpu.VMEM((6, 2 * KEPT_COLS, 512), F32),
        ],
        name="grid",
    )(came, groups, *z_table, *x_inverse, *x_forward)
    came = lax.all_to_all(back, ALL, 0, 0, tiled=True)

    means = sums[:4, 0] / (GMODES * KX * N)
    power_here = lax.dynamic_slice_in_dim(power, grp * 2, 2)
    damping_here = lax.dynamic_slice_in_dim(damping, grp * 2, 2)
    forcing = (power_here - means[:2]) / (2.0 * (means[2:] + EPSILON))
    reals = jnp.concatenate([forcing, damping_here])
    integers = jnp.concatenate([jnp.stack([grp, slab]).astype(jnp.int32), cutoffs])
    made = pl.pallas_call(
        update_kernel,
        out_shape=jax.ShapeDtypeStruct((16, 128, N), F32),
        in_specs=[SM, SM] + [VM] * 5,
        out_specs=VM,
        name="update",
    )(integers, reals, came.reshape(128 * ROWS_BACK, 128), rows, groups, *y_forward)
    return made.reshape(4, 4, 2, 64, N).transpose(0, 2, 3, 1, 4)


def solution(mesh):
    finer = Mesh(
        mesh.devices.reshape(mesh.shape["grp"], 4, 4, 2), ("grp", "slab_0", "slab_1", "slab_2")
    )
    return jax.shard_map(
        shards,
        mesh=finer,
        in_specs=(P(None, None, "grp", SLAB, None), P(), P(), P(), P()),
        out_specs=P(None, None, "grp", SLAB, None),
        check_vma=False,
    )
```

```python
import functools
import math

import jax
import jax.numpy as jnp
import numpy as np
from jax import lax
from jax.experimental import pallas as pl
from jax.experimental.pallas import tpu as pltpu
from jax.sharding import Mesh
from jax.sharding import PartitionSpec as P

N = 256
GROUPS = 8
KX = 128
GMODES = 32
KEPT_COLS = 88
SLAB = ("slab_0", "slab_1", "slab_2")
ALL = ("grp",) + SLAB
HALF = N // 2

TWO_PI = 6.283185307179586
WAVE = TWO_PI / N
TIME_STEP = 0.25
CORIOLIS = 1.0
BRUNT_SQUARED = 2.0
EPSILON = 1e-06
SCALE = 1.0 / 4096.0
FIELDS_OUT = 6
FIELDS_BACK = 5
ROWS_OUT = 8 * FIELDS_OUT
ROWS_BACK = 8 * FIELDS_BACK + 1

SEND_MIB = 24
GRID_MIB = 40
UPDATE_MIB = 24

F32 = jnp.float32
BF16 = jnp.bfloat16


def halves(table):
    high = table.astype(np.float32).astype(jnp.bfloat16)
    low = (table - high.astype(np.float64)).astype(np.float32).astype(jnp.bfloat16)
    return jnp.asarray(high), jnp.asarray(low)


def angle(rows, cols):
    return 2.0 * np.pi / N * (np.outer(rows, cols) % N).astype(np.float64)


def signed(index):
    return np.where(index < N // 2, index, index - N)


def folded():
    theta = angle(np.arange(HALF), np.arange(N))
    cosine, sine = np.cos(theta), np.sin(theta)
    odd = np.arange(N) % 2
    cosine[0], sine[0] = 1 - odd, odd
    return np.stack([cosine, sine])


def tables():
    points = np.arange(N)
    pair = folded()
    wave = (WAVE * signed(points))[None, None, :]
    y_inverse = np.concatenate([pair, wave * pair]).reshape(4 * HALF, N)
    fold = pair.reshape(N, N)
    theta = angle(points, np.arange(KX))
    weight = np.where(np.arange(KX) == 0, 1.0, 2.0) * SCALE
    x_inverse = np.concatenate([np.cos(theta) * weight, -np.sin(theta) * weight], axis=1)
    theta = theta.T[:KEPT_COLS]
    x_forward = np.concatenate([np.cos(theta), -np.sin(theta)], axis=0) * SCALE
    return [halves(t) for t in (y_inverse, fold.T.copy(), x_inverse, x_forward, fold)]


def split(value):
    high = value.astype(BF16)
    low = (value - high.astype(F32)).astype(BF16)
    return high, low


def product(left, right, dims):
    def one(a, b):
        return lax.dot_general(a, b, (dims, ((), ())), preferred_element_type=F32)

    return one(left[0], right[0]) + (one(left[0], right[1]) + one(left[1], right[0]))


def slot_rows(group_row, slots):
    member = (lax.broadcasted_iota(jnp.int32, (GROUPS, N), 0) == group_row).astype(F32)
    earlier = (
        lax.broadcasted_iota(jnp.int32, (N, N), 0) < lax.broadcasted_iota(jnp.int32, (N, N), 1)
    ).astype(F32)
    count = jnp.dot(member.astype(BF16), earlier.astype(BF16), preferred_element_type=F32)
    first = (GMODES * lax.broadcasted_iota(jnp.int32, (GROUPS, N), 0)).astype(F32)
    place = jnp.sum(member * (first + count), axis=0, keepdims=True).astype(jnp.int32)
    return slots == place


def signed_row(shape):
    index = lax.broadcasted_iota(jnp.int32, shape, len(shape) - 1)
    return jnp.where(index < N // 2, index, index - N)


def lanes(shape):
    return lax.broadcasted_iota(jnp.int32, shape, len(shape) - 1)


def send_kernel(state, w_high, w_low, sent, sums):
    sign = jnp.where(lanes((HALF, 128)) < 64, -1.0, 1.0).astype(F32)
    top = lax.broadcasted_iota(jnp.int32, (HALF, 128), 0) == 0
    flux = jnp.zeros((128, N), F32)
    energy = jnp.zeros((128, N), F32)

    def put(slot, x, even, odd):
        for low, value in ((0, even + odd), (1, even - odd)):
            sent[pl.ds(slot * 8 + low * 4 + x, 128, stride=ROWS_OUT), :] = value

    for pair in range(2):
        pieces = []
        for f in range(4):
            rows = []
            for x in (2 * pair, 2 * pair + 1):
                for part in range(2):
                    rows.append(
                        jnp.concatenate(
                            [
                                state[f * 2 + part, pl.ds(h * 4 + x, 64, stride=8), :]
                                for h in range(2)
                            ],
                            axis=1,
                        )
                    )
            pieces.append(jnp.concatenate(rows, axis=0))
        flow_x, flow_y, flow_z, buoyant = pieces
        moved = flow_z * buoyant
        held = 0.5 * (
            flow_x * flow_x
            + flow_y * flow_y
            + flow_z * flow_z
            + buoyant * buoyant * (1.0 / BRUNT_SQUARED)
        )
        flux = flux + (moved[:128] + moved[128:])
        energy = energy + (held[:128] + held[128:])
        for f in range(4):
            derived = {0: 4, 2: 5}.get(f)
            count = 512 if derived else 256
            made = product((w_high[:count], w_low[:count]), split(pieces[f]), ((1,), (1,)))
            for k in range(2):
                x = pair * 2 + k
                cols = slice(k * 128, (k + 1) * 128)
                even, odd = made[0:128, cols], made[128:256, cols]
                put(f, x, even, jnp.where(top, odd, sign * pltpu.roll(odd, 64, 1)))
                if derived:
                    even, odd = made[256:384, cols], made[384:512, cols]
                    even = sign * pltpu.roll(even, 64, 1)
                    put(derived, x, even, jnp.where(top, sign * pltpu.roll(odd, 64, 1), -odd))

    quarter = lanes((1, 128)) // 32
    total = jnp.zeros((1, 128), F32)
    for k, value in enumerate((flux, energy)):
        for which in range(2):
            low = which * GMODES
            part = jnp.sum(value[low : low + 32] + value[64 + low : 96 + low], axis=0, keepdims=True)
            part = part[:, :128] + part[:, 128:]
            part = part + pltpu.roll(part, 64, 1)
            part = part + pltpu.roll(part, 32, 1)
            total = jnp.where(quarter == 2 * k + which, part, total)
    sums[...] = jnp.broadcast_to(total, (8, 128))


def grid_kernel(
    came,
    sums,
    groups,
    zt_high,
    zt_low,
    xi_high,
    xi_low,
    xf_high,
    xf_low,
    sent,
    wz_high,
    wz_low,
    rows_z,
    planes,
    lines,
):
    picked = slot_rows(groups[...], lax.broadcasted_iota(jnp.int32, (N, N), 0)).astype(BF16)
    for table, out in ((zt_high, wz_high), (zt_low, wz_low)):
        out[...] = jnp.dot(picked, table[...], preferred_element_type=F32).astype(BF16)
    kz = lax.dot_general(
        signed_row((8, N)).astype(F32).astype(BF16),
        picked,
        (((1,), (1,)), ((), ())),
        preferred_element_type=F32,
    )
    kz = kz[0:1, :] * WAVE
    kx = (lax.broadcasted_iota(jnp.int32, (N, 1), 0) % 128).astype(F32) * WAVE
    weights = (wz_high[...], wz_low[...])

    def separate(first, second):
        low = lanes(first.shape) < 64
        return (
            jnp.where(low, first, pltpu.roll(second, 64, 1)),
            jnp.where(low, pltpu.roll(first, 64, 1), second),
        )

    upper = lax.broadcasted_iota(jnp.int32, (16, 8, 128), 1) < 4

    def field(f):
        pieces = []
        for g in range(4):
            tiles = came[g * 32 : (g + 1) * 32, f * 8 : (f + 1) * 8, :].reshape(16, 2, 8, 128)
            even, odd = tiles[:, 0], tiles[:, 1]
            first = jnp.where(upper, even, pltpu.roll(odd, 4, 1))
            second = jnp.where(upper, pltpu.roll(even, 4, 1), odd)
            pieces.append(
                jnp.concatenate([first.reshape(128, 128), second.reshape(128, 128)], axis=0)
            )
        near, far = separate(pieces[0], pieces[1]), separate(pieces[2], pieces[3])
        return tuple(jnp.concatenate([near[k], far[k]], axis=1) for k in range(2))

    start = lanes((N, HALF)) == 0

    def vertical(value, slot):
        made = product(split(jnp.concatenate(value, axis=0)), weights, ((1,), (0,)))
        even = (made[:N, :HALF], made[N:, :HALF])
        odd = (made[:N, HALF:], made[N:, HALF:])
        turned = (jnp.where(start, odd[0], -odd[1]), jnp.where(start, odd[1], odd[0]))
        for part in range(2):
            for k, both in enumerate((even[part] + turned[part], even[part] - turned[part])):
                for plane in range(2):
                    col = plane * N + k * HALF
                    rows_z[slot, part * 128 : (part + 1) * 128, col : col + HALF] = both[
                        plane * 128 : (plane + 1) * 128
                    ]

    flow_x = field(0)
    vertical(flow_x, 0)
    flow_z = field(2)
    vertical(flow_z, 2)
    vertical(
        (kx * flow_z[1] - kz * flow_x[1], kz * flow_x[0] - kx * flow_z[0]),
        5,
    )
    flow_y = field(1)
    vertical(flow_y, 1)
    slope = field(5)
    vertical((slope[0] + kz * flow_y[1], slope[1] - kz * flow_y[0]), 4)
    slope = field(4)
    vertical((-(kx * flow_y[1]) - slope[0], kx * flow_y[0] - slope[1]), 6)
    vertical(field(3), 3)

    x_inverse = (xi_high[...], xi_low[...])
    for slot in range(7):
        planes[slot] = product(x_inverse, split(rows_z[slot]), ((1,), (0,)))

    x_forward = (xf_high[...], xf_low[...])
    start_kept = lanes((KEPT_COLS, HALF)) == 0

    def horizontal(value, slot):
        pieces = []
        for plane in range(2):
            near = value[:, plane * N : plane * N + HALF]
            far = value[:, plane * N + HALF : (plane + 1) * N]
            pieces += [near + far, near - far]
        made = product(x_forward, split(jnp.concatenate(pieces, axis=1)), ((1,), (0,)))
        for plane in range(2):
            col = plane * N
            plus = made[:, col : col + HALF]
            odd_real = made[:KEPT_COLS, col + HALF : col + N]
            odd_imag = made[KEPT_COLS:, col + HALF : col + N]
            real, imag = plane * KEPT_COLS, (2 + plane) * KEPT_COLS
            lines[slot, real : real + KEPT_COLS, :HALF] = plus[:KEPT_COLS]
            lines[slot, imag : imag + KEPT_COLS, :HALF] = plus[KEPT_COLS:]
            lines[slot, real : real + KEPT_COLS, HALF:] = jnp.where(start_kept, odd_real, odd_imag)
            lines[slot, imag : imag + KEPT_COLS, HALF:] = jnp.where(
                start_kept, odd_imag, -odd_real
            )

    u, v, w, b, ox, oy, oz = range(7)
    horizontal(planes[v] * planes[oz] - planes[w] * planes[oy], 0)
    horizontal(planes[w] * planes[ox] - planes[u] * planes[oz], 1)
    horizontal(planes[u] * planes[oy] - planes[v] * planes[ox], 2)
    horizontal(planes[u] * planes[b], 3)
    horizontal(planes[v] * planes[b], 4)
    horizontal(planes[w] * planes[b], 5)

    row = lax.broadcasted_iota(jnp.int32, (4 * KEPT_COLS, 1), 0)
    kx_kept = (row % KEPT_COLS).astype(F32) * WAVE
    upper_kept = lax.broadcasted_iota(jnp.int32, (11, 8, 128), 1) < 4

    def slots(value):
        return product(split(value), weights, ((1,), (1,)))

    for g in range(4):
        low = (g * 32 + 22) * ROWS_BACK
        sent[low : low + 10 * ROWS_BACK] = jnp.zeros((10 * ROWS_BACK, 128), F32)

    def put(value, f):
        for pair in range(2):
            cols = slice(pair * 128, (pair + 1) * 128)
            both = separate(value[: 2 * KEPT_COLS, cols], value[2 * KEPT_COLS :, cols])
            for k in range(2):
                g = 2 * pair + k
                first = both[k][:KEPT_COLS].reshape(11, 8, 128)
                second = both[k][KEPT_COLS:].reshape(11, 8, 128)
                even = jnp.where(upper_kept, first, pltpu.roll(second, 4, 1))
                odd = jnp.where(upper_kept, pltpu.roll(first, 4, 1), second)
                for j in range(11):
                    low = (g * 32 + 2 * j) * ROWS_BACK + f * 8
                    sent[low : low + 8, :] = even[j]
                    sent[low + ROWS_BACK : low + ROWS_BACK + 8, :] = odd[j]

    for k in range(3):
        put(slots(lines[k]), k)
    put(kx_kept * slots(lines[3]) + kz * slots(lines[5]), 3)
    put(slots(lines[4]), 4)
    sent[pl.ds(8 * FIELDS_BACK, 128, stride=ROWS_BACK), :] = jnp.broadcast_to(
        sums[0:1, :], (128, 128)
    )


def update_kernel(cutoffs, damping_of, power_of, came, state, groups, yf_high, yf_low, made_state):
    grp = lax.axis_index("grp")
    slab = lax.axis_index(SLAB)
    index = lax.broadcasted_iota(jnp.int32, (64, N), 0)
    picked = slot_rows(groups[...], index + grp * 64)
    mode_z = jnp.sum(jnp.where(picked, signed_row((64, N)), 0), axis=1, keepdims=True)
    mode_y = signed_row((1, N))
    slot = lax.broadcasted_iota(jnp.int32, (64, 1), 0)
    source_grp = lax.broadcasted_iota(jnp.int32, (128, 128), 0) // 32
    total = came[pl.ds(8 * FIELDS_BACK, 128, stride=ROWS_BACK), :]
    total = jnp.sum(jnp.where(source_grp == grp, total, 0.0), axis=0, keepdims=True)
    quarter = lanes((1, 128)) // 32
    means = [
        jnp.sum(jnp.where(quarter == k, total, 0.0), axis=1, keepdims=True) / (GMODES * KX * N)
        for k in range(4)
    ]
    forcings = [
        (power_of[grp * 2 + k] - means[k]) / (2.0 * (means[2 + k] + EPSILON)) for k in range(2)
    ]
    forcing = jnp.where(slot < GMODES, forcings[0], forcings[1])
    damping = jnp.where(slot < GMODES, damping_of[grp * 2], damping_of[grp * 2 + 1])
    wave_z = mode_z.astype(F32) * WAVE
    wave_y = mode_y.astype(F32) * WAVE
    kept_zy = (96 * jnp.abs(mode_z) <= cutoffs[2] * N) & (96 * jnp.abs(mode_y) <= cutoffs[1] * N)
    table = (yf_high[...], yf_low[...])
    wave_zy = wave_y * wave_y + wave_z * wave_z
    grown = 1.0 + TIME_STEP * forcing
    rotation = TIME_STEP * CORIOLIS
    top = lax.broadcasted_iota(jnp.int32, (128, 128), 0) == 0
    sign = jnp.where(lanes((128, 128)) < 64, 1.0, -1.0).astype(F32)
    for x in range(4):
        mode_x = slab * 4 + x
        wave_x = mode_x.astype(F32) * WAVE
        kept = kept_zy & (96 * mode_x <= cutoffs[0] * N)

        def spectral(f):
            near, far = (
                came[pl.ds(f * 8 + low * 4 + x, 128, stride=ROWS_BACK), :] for low in range(2)
            )
            odd = near - far
            odd = jnp.where(top, odd, sign * pltpu.roll(odd, 64, 1))
            both = jnp.concatenate([(near + far).T, odd.T], axis=1)
            got = product(split(both), table, ((1,), (0,)))
            return got[0:64], got[64:128]

        moments = [spectral(f) for f in range(3)]
        partial_b = spectral(3)
        flux_y = spectral(4)
        source = [partial_b[k] + wave_y * flux_y[k] for k in range(2)]
        sources = (source[1], -source[0])
        wave_sq = wave_x * wave_x + wave_zy
        implicit = 1.0 + TIME_STEP * damping * wave_sq
        square = implicit * implicit
        first = 1.0 / (square + rotation * rotation)
        second = 1.0 / (square + TIME_STEP * TIME_STEP * BRUNT_SQUARED)
        inverse_sq = 1.0 / jnp.where(wave_sq == 0, 1.0, wave_sq)
        for k in range(2):
            flows = [
                jnp.concatenate(
                    [state[f * 2 + k, pl.ds(h * 4 + x, 64, stride=8), :] for h in range(2)], axis=1
                )
                for f in range(4)
            ]
            right = [
                flows[f] * grown + jnp.where(kept, TIME_STEP * moments[f][k], 0.0)
                for f in range(3)
            ]
            right_b = flows[3] + jnp.where(kept, TIME_STEP * sources[k], 0.0)
            new_x = (implicit * right[0] + rotation * right[1]) * first
            new_y = (implicit * right[1] - rotation * right[0]) * first
            new_z = (implicit * right[2] + TIME_STEP * right_b) * second
            new_b = (implicit * right_b - TIME_STEP * BRUNT_SQUARED * right[2]) * second
            inner = (wave_x * new_x + wave_y * new_y + wave_z * new_z) * inverse_sq
            made = (new_x - wave_x * inner, new_y - wave_y * inner, new_z - wave_z * inner, new_b)
            for f in range(4):
                for h in range(2):
                    made_state[f * 2 + k, pl.ds(h * 4 + x, 64, stride=8), :] = made[f][
                        :, h * 128 : (h + 1) * 128
                    ]


VM = pl.BlockSpec(memory_space=pltpu.VMEM)
SM = pl.BlockSpec(memory_space=pltpu.SMEM)


def granted(mebibytes):
    return pltpu.CompilerParams(vmem_limit_bytes=mebibytes << 20)


def shards(state, kz_group, cutoffs, damping, power):
    y_inverse, z_table, x_inverse, x_forward, y_forward = tables()
    groups = kz_group.reshape(1, N)
    rows = state.reshape(4, 2, 64, 4, 2, 128).transpose(0, 1, 2, 4, 3, 5).reshape(8, 512, 128)

    sent, sums = pl.pallas_call(
        send_kernel,
        out_shape=(
            jax.ShapeDtypeStruct((128 * ROWS_OUT, 128), F32),
            jax.ShapeDtypeStruct((8, 128), F32),
        ),
        in_specs=[VM] * 3,
        out_specs=(VM, VM),
        compiler_params=granted(SEND_MIB),
        name="send",
    )(rows, *y_inverse)
    came = lax.all_to_all(sent.reshape(128, ROWS_OUT, 128), ALL, 0, 0, tiled=True)

    back = pl.pallas_call(
        grid_kernel,
        out_shape=jax.ShapeDtypeStruct((128 * ROWS_BACK, 128), F32),
        in_specs=[VM] * 9,
        out_specs=VM,
        scratch_shapes=[
            pltpu.VMEM((N, N), BF16),
            pltpu.VMEM((N, N), BF16),
            pltpu.VMEM((7, 256, 512), F32),
            pltpu.VMEM((7, 256, 512), F32),
            pltpu.VMEM((6, 4 * KEPT_COLS, N), F32),
        ],
        compiler_params=granted(GRID_MIB),
        name="grid",
    )(came, sums, groups, *z_table, *x_inverse, *x_forward)
    came = lax.all_to_all(back.reshape(128, 1, ROWS_BACK * 128), ALL, 0, 0, tiled=True)

    made = pl.pallas_call(
        update_kernel,
        out_shape=jax.ShapeDtypeStruct((8, 512, 128), F32),
        in_specs=[SM] * 3 + [VM] * 5,
        out_specs=VM,
        compiler_params=granted(UPDATE_MIB),
        name="update",
    )(cutoffs, damping, power, came.reshape(128 * ROWS_BACK, 128), rows, groups, *y_forward)
    made = made.reshape(4, 2, 64, 2, 4, 128).transpose(0, 1, 2, 4, 3, 5)
    return made.reshape(4, 2, 64, 4, N)


def solution(mesh):
    finer = Mesh(
        mesh.devices.reshape(mesh.shape["grp"], 4, 4, 2), ("grp", "slab_0", "slab_1", "slab_2")
    )
    return jax.shard_map(
        shards,
        mesh=finer,
        in_specs=(P(None, None, "grp", SLAB, None), P(), P(), P(), P()),
        out_specs=P(None, None, "grp", SLAB, None),
        check_vma=False,
    )
```

```python
import functools
import math

import jax
import jax.numpy as jnp
import numpy as np
from jax import lax
from jax.experimental import pallas as pl
from jax.experimental.pallas import tpu as pltpu
from jax.sharding import Mesh
from jax.sharding import PartitionSpec as P

N = 256
GROUPS = 8
KX = 128
GMODES = 32
KEPT_COLS = 88
SLAB = ("slab_0", "slab_1", "slab_2")
ALL = ("grp",) + SLAB
HALF = N // 2

TWO_PI = 6.283185307179586
WAVE = TWO_PI / N
TIME_STEP = 0.25
CORIOLIS = 1.0
BRUNT_SQUARED = 2.0
EPSILON = 1e-06
SCALE = 1.0 / 4096.0
FIELDS_OUT = 6
FIELDS_BACK = 5
ROWS_OUT = 8 * FIELDS_OUT
ROWS_BACK = 8 * FIELDS_BACK + 1

SEND_MIB = 24
GRID_MIB = 40
UPDATE_MIB = 28

F32 = jnp.float32
BF16 = jnp.bfloat16


def halves(table):
    high = table.astype(np.float32).astype(jnp.bfloat16)
    low = (table - high.astype(np.float64)).astype(np.float32).astype(jnp.bfloat16)
    return jnp.asarray(high), jnp.asarray(low)


def angle(rows, cols):
    return 2.0 * np.pi / N * (np.outer(rows, cols) % N).astype(np.float64)


def signed(index):
    return np.where(index < N // 2, index, index - N)


def folded():
    theta = angle(np.arange(HALF), np.arange(N))
    cosine, sine = np.cos(theta), np.sin(theta)
    odd = np.arange(N) % 2
    cosine[0], sine[0] = 1 - odd, odd
    return np.stack([cosine, sine])


def tables():
    points = np.arange(N)
    pair = folded()
    wave = (WAVE * signed(points))[None, None, :]
    y_inverse = np.concatenate([pair, wave * pair]).reshape(4 * HALF, N)
    fold = pair.reshape(N, N)
    theta = angle(points, np.arange(KX))
    weight = np.where(np.arange(KX) == 0, 1.0, 2.0) * SCALE
    x_inverse = np.concatenate([np.cos(theta) * weight, -np.sin(theta) * weight], axis=1)
    theta = theta.T[:KEPT_COLS]
    x_forward = np.concatenate([np.cos(theta), -np.sin(theta)], axis=0) * SCALE
    return [halves(t) for t in (y_inverse, fold.T.copy(), x_inverse, x_forward, fold)]


def split(value):
    high = value.astype(BF16)
    low = (value - high.astype(F32)).astype(BF16)
    return high, low


def product(left, right, dims):
    def one(a, b):
        return lax.dot_general(a, b, (dims, ((), ())), preferred_element_type=F32)

    return one(left[0], right[0]) + (one(left[0], right[1]) + one(left[1], right[0]))


def slot_rows(group_row, slots):
    member = (lax.broadcasted_iota(jnp.int32, (GROUPS, N), 0) == group_row).astype(F32)
    earlier = (
        lax.broadcasted_iota(jnp.int32, (N, N), 0) < lax.broadcasted_iota(jnp.int32, (N, N), 1)
    ).astype(F32)
    count = jnp.dot(member.astype(BF16), earlier.astype(BF16), preferred_element_type=F32)
    first = (GMODES * lax.broadcasted_iota(jnp.int32, (GROUPS, N), 0)).astype(F32)
    place = jnp.sum(member * (first + count), axis=0, keepdims=True).astype(jnp.int32)
    return slots == place


def signed_row(shape):
    index = lax.broadcasted_iota(jnp.int32, shape, len(shape) - 1)
    return jnp.where(index < N // 2, index, index - N)


def lanes(shape):
    return lax.broadcasted_iota(jnp.int32, shape, len(shape) - 1)


def fill_factors(cutoffs, damping_of, groups, factors):
    grp = lax.axis_index("grp")
    slab = lax.axis_index(SLAB)
    here = slot_rows(groups[...], lax.broadcasted_iota(jnp.int32, (64, N), 0) + grp * 64)
    mode_z = jnp.sum(jnp.where(here, signed_row((64, N)), 0), axis=1, keepdims=True)
    mode_y = signed_row((1, N))
    slot = lax.broadcasted_iota(jnp.int32, (64, 1), 0)
    damping = jnp.where(slot < GMODES, damping_of[grp * 2], damping_of[grp * 2 + 1])
    wave_z = mode_z.astype(F32) * WAVE
    wave_y = mode_y.astype(F32) * WAVE
    kept_zy = (96 * jnp.abs(mode_z) <= cutoffs[2] * N) & (96 * jnp.abs(mode_y) <= cutoffs[1] * N)
    wave_zy = wave_y * wave_y + wave_z * wave_z
    rotation = TIME_STEP * CORIOLIS
    for x in range(4):
        mode_x = slab * 4 + x
        wave_x = mode_x.astype(F32) * WAVE
        kept = kept_zy & (96 * mode_x <= cutoffs[0] * N)
        wave_sq = wave_x * wave_x + wave_zy
        implicit = 1.0 + TIME_STEP * damping * wave_sq
        square = implicit * implicit
        first = 1.0 / (square + rotation * rotation)
        second = 1.0 / (square + TIME_STEP * TIME_STEP * BRUNT_SQUARED)
        factors[0, x] = implicit * first
        factors[1, x] = rotation * first
        factors[2, x] = implicit * second
        factors[3, x] = TIME_STEP * second
        factors[4, x] = 1.0 / jnp.where(wave_sq == 0, 1.0, wave_sq)
        factors[5, x] = jnp.where(kept, TIME_STEP, 0.0)
    factors[6, 0] = jnp.broadcast_to(wave_z, (64, N))


def send_kernel(
    cutoffs_far,
    damping_far,
    groups_far,
    state_far,
    w_high_far,
    w_low_far,
    sent,
    sums,
    factors,
    cutoffs,
    damping_of,
    groups,
    state,
    w_high,
    w_low,
    sems,
):
    copies = {}

    def fetch(key, source, target, k):
        copies[key] = pltpu.make_async_copy(source, target, sems.at[k])
        copies[key].start()

    small = ((groups_far, groups), (cutoffs_far, cutoffs), (damping_far, damping_of))
    for k, (source, target) in enumerate(small):
        fetch(k, source, target, 8 + k)
    order = (1, 0, 2, 3)
    for k, low in enumerate((0, N)):
        rows = pl.ds(low, N)
        if k == 0:
            fetch("high0", w_high_far.at[rows], w_high.at[rows], 0)
            fetch("state1", state_far.at[pl.ds(2, 2)], state.at[pl.ds(2, 2)], 1)
            fetch("low0", w_low_far.at[rows], w_low.at[rows], 2)
        else:
            fetch("high1", w_high_far.at[rows], w_high.at[rows], 3)
            fetch("low1", w_low_far.at[rows], w_low.at[rows], 4)
    for k, f in enumerate(order[1:]):
        rows = pl.ds(2 * f, 2)
        fetch("state" + str(f), state_far.at[rows], state.at[rows], 5 + k)

    for k in range(3):
        copies[k].wait()
    fill_factors(cutoffs, damping_of, groups, factors)

    sign = jnp.where(lanes((HALF, 128)) < 64, -1.0, 1.0).astype(F32)
    top = lax.broadcasted_iota(jnp.int32, (HALF, 128), 0) == 0
    flux = jnp.zeros((128, N), F32)
    energy = jnp.zeros((128, N), F32)

    def put(slot, x, even, odd):
        for low, value in ((0, even + odd), (1, even - odd)):
            sent[pl.ds(slot * 8 + low * 4 + x, 128, stride=ROWS_OUT), :] = value

    def piece(f, pair):
        rows = []
        for x in (2 * pair, 2 * pair + 1):
            for part in range(2):
                rows.append(
                    jnp.concatenate(
                        [state[f * 2 + part, pl.ds(h * 4 + x, 64, stride=8), :] for h in range(2)],
                        axis=1,
                    )
                )
        return jnp.concatenate(rows, axis=0)

    for f in order:
        if f == 1:
            for key in ("high0", "low0", "high1", "low1", "state1", "state0"):
                copies[key].wait()
        if f == 2:
            copies["state2"].wait()
            copies["state3"].wait()
        derived = {0: 4, 2: 5}.get(f)
        count = 512 if derived else 256
        share = 0.5 / BRUNT_SQUARED if f == 3 else 0.5
        for pair in range(2):
            value = piece(f, pair)
            square = share * (value * value)
            energy = energy + (square[:128] + square[128:])
            if f == 3:
                moved = value * piece(2, pair)
                flux = flux + (moved[:128] + moved[128:])
            made = product((w_high[:count], w_low[:count]), split(value), ((1,), (1,)))
            for k in range(2):
                x = pair * 2 + k
                cols = slice(k * 128, (k + 1) * 128)
                even, odd = made[0:128, cols], made[128:256, cols]
                put(f, x, even, jnp.where(top, odd, sign * pltpu.roll(odd, 64, 1)))
                if derived:
                    even, odd = made[256:384, cols], made[384:512, cols]
                    even = sign * pltpu.roll(even, 64, 1)
                    put(derived, x, even, jnp.where(top, sign * pltpu.roll(odd, 64, 1), -odd))

    quarter = lanes((1, 128)) // 32
    total = jnp.zeros((1, 128), F32)
    for k, value in enumerate((flux, energy)):
        for which in range(2):
            low = which * GMODES
            part = jnp.sum(value[low : low + 32] + value[64 + low : 96 + low], axis=0, keepdims=True)
            part = part[:, :128] + part[:, 128:]
            part = part + pltpu.roll(part, 64, 1)
            part = part + pltpu.roll(part, 32, 1)
            total = jnp.where(quarter == 2 * k + which, part, total)
    sums[...] = jnp.broadcast_to(total, (8, 128))


def grid_kernel(
    came,
    sums,
    groups,
    zt_high,
    zt_low,
    xi_high,
    xi_low,
    xf_high,
    xf_low,
    sent,
    wz_high,
    wz_low,
    rows_z,
    planes,
    lines,
):
    picked = slot_rows(groups[...], lax.broadcasted_iota(jnp.int32, (N, N), 0)).astype(BF16)
    for table, out in ((zt_high, wz_high), (zt_low, wz_low)):
        out[...] = jnp.dot(picked, table[...], preferred_element_type=F32).astype(BF16)
    kz = lax.dot_general(
        signed_row((8, N)).astype(F32).astype(BF16),
        picked,
        (((1,), (1,)), ((), ())),
        preferred_element_type=F32,
    )
    kz = kz[0:1, :] * WAVE
    kx = (lax.broadcasted_iota(jnp.int32, (N, 1), 0) % 128).astype(F32) * WAVE
    weights = (wz_high[...], wz_low[...])

    def separate(first, second):
        low = lanes(first.shape) < 64
        return (
            jnp.where(low, first, pltpu.roll(second, 64, 1)),
            jnp.where(low, pltpu.roll(first, 64, 1), second),
        )

    upper = lax.broadcasted_iota(jnp.int32, (16, 8, 128), 1) < 4

    def field(f):
        pieces = []
        for g in range(4):
            tiles = came[g * 32 : (g + 1) * 32, f * 8 : (f + 1) * 8, :].reshape(16, 2, 8, 128)
            even, odd = tiles[:, 0], tiles[:, 1]
            first = jnp.where(upper, even, pltpu.roll(odd, 4, 1))
            second = jnp.where(upper, pltpu.roll(even, 4, 1), odd)
            pieces.append(
                jnp.concatenate([first.reshape(128, 128), second.reshape(128, 128)], axis=0)
            )
        near, far = separate(pieces[0], pieces[1]), separate(pieces[2], pieces[3])
        return tuple(jnp.concatenate([near[k], far[k]], axis=1) for k in range(2))

    start = lanes((N, HALF)) == 0

    def vertical(value, slot):
        made = product(split(jnp.concatenate(value, axis=0)), weights, ((1,), (0,)))
        even = (made[:N, :HALF], made[N:, :HALF])
        odd = (made[:N, HALF:], made[N:, HALF:])
        turned = (jnp.where(start, odd[0], -odd[1]), jnp.where(start, odd[1], odd[0]))
        for part in range(2):
            for k, both in enumerate((even[part] + turned[part], even[part] - turned[part])):
                for plane in range(2):
                    col = plane * N + k * HALF
                    rows_z[slot, part * 128 : (part + 1) * 128, col : col + HALF] = both[
                        plane * 128 : (plane + 1) * 128
                    ]

    flow_x = field(0)
    vertical(flow_x, 0)
    flow_z = field(2)
    vertical(flow_z, 2)
    vertical(
        (kx * flow_z[1] - kz * flow_x[1], kz * flow_x[0] - kx * flow_z[0]),
        5,
    )
    flow_y = field(1)
    vertical(flow_y, 1)
    slope = field(5)
    vertical((slope[0] + kz * flow_y[1], slope[1] - kz * flow_y[0]), 4)
    slope = field(4)
    vertical((-(kx * flow_y[1]) - slope[0], kx * flow_y[0] - slope[1]), 6)
    vertical(field(3), 3)

    x_inverse = (xi_high[...], xi_low[...])
    for slot in range(7):
        planes[slot] = product(x_inverse, split(rows_z[slot]), ((1,), (0,)))

    x_forward = (xf_high[...], xf_low[...])
    start_kept = lanes((KEPT_COLS, HALF)) == 0

    def horizontal(value, slot):
        pieces = []
        for plane in range(2):
            near = value[:, plane * N : plane * N + HALF]
            far = value[:, plane * N + HALF : (plane + 1) * N]
            pieces += [near + far, near - far]
        made = product(x_forward, split(jnp.concatenate(pieces, axis=1)), ((1,), (0,)))
        for plane in range(2):
            col = plane * N
            plus = made[:, col : col + HALF]
            odd_real = made[:KEPT_COLS, col + HALF : col + N]
            odd_imag = made[KEPT_COLS:, col + HALF : col + N]
            real, imag = plane * KEPT_COLS, (2 + plane) * KEPT_COLS
            lines[slot, real : real + KEPT_COLS, :HALF] = plus[:KEPT_COLS]
            lines[slot, imag : imag + KEPT_COLS, :HALF] = plus[KEPT_COLS:]
            lines[slot, real : real + KEPT_COLS, HALF:] = jnp.where(start_kept, odd_real, odd_imag)
            lines[slot, imag : imag + KEPT_COLS, HALF:] = jnp.where(
                start_kept, odd_imag, -odd_real
            )

    u, v, w, b, ox, oy, oz = range(7)
    horizontal(planes[v] * planes[oz] - planes[w] * planes[oy], 0)
    horizontal(planes[w] * planes[ox] - planes[u] * planes[oz], 1)
    horizontal(planes[u] * planes[oy] - planes[v] * planes[ox], 2)
    horizontal(planes[u] * planes[b], 3)
    horizontal(planes[v] * planes[b], 4)
    horizontal(planes[w] * planes[b], 5)

    row = lax.broadcasted_iota(jnp.int32, (4 * KEPT_COLS, 1), 0)
    kx_kept = (row % KEPT_COLS).astype(F32) * WAVE
    upper_kept = lax.broadcasted_iota(jnp.int32, (11, 8, 128), 1) < 4

    def slots(value):
        return product(split(value), weights, ((1,), (1,)))

    for g in range(4):
        low = (g * 32 + 22) * ROWS_BACK
        sent[low : low + 10 * ROWS_BACK] = jnp.zeros((10 * ROWS_BACK, 128), F32)

    def put(value, f):
        for pair in range(2):
            cols = slice(pair * 128, (pair + 1) * 128)
            both = separate(value[: 2 * KEPT_COLS, cols], value[2 * KEPT_COLS :, cols])
            for k in range(2):
                g = 2 * pair + k
                first = both[k][:KEPT_COLS].reshape(11, 8, 128)
                second = both[k][KEPT_COLS:].reshape(11, 8, 128)
                even = jnp.where(upper_kept, first, pltpu.roll(second, 4, 1))
                odd = jnp.where(upper_kept, pltpu.roll(first, 4, 1), second)
                for j in range(11):
                    low = (g * 32 + 2 * j) * ROWS_BACK + f * 8
                    sent[low : low + 8, :] = even[j]
                    sent[low + ROWS_BACK : low + ROWS_BACK + 8, :] = odd[j]

    for k in range(3):
        put(slots(lines[k]), k)
    put(kx_kept * slots(lines[3]) + kz * slots(lines[5]), 3)
    put(slots(lines[4]), 4)
    sent[pl.ds(8 * FIELDS_BACK, 128, stride=ROWS_BACK), :] = jnp.broadcast_to(
        sums[0:1, :], (128, 128)
    )


BLOCK = 8


def update_kernel(
    power_of, came, state, factors, yf_high, yf_low, made_far, left_high, left_low, got, made_state, sems
):
    grp = lax.axis_index("grp")
    slab = lax.axis_index(SLAB)
    source_grp = lax.broadcasted_iota(jnp.int32, (128, 128), 0) // 32
    total = came[pl.ds(8 * FIELDS_BACK, 128, stride=ROWS_BACK), :]
    total = jnp.sum(jnp.where(source_grp == grp, total, 0.0), axis=0, keepdims=True)
    quarter = lanes((1, 128)) // 32
    means = [
        jnp.sum(jnp.where(quarter == k, total, 0.0), axis=1, keepdims=True) / (GMODES * KX * N)
        for k in range(4)
    ]
    grown = [
        1.0
        + TIME_STEP * ((power_of[grp * 2 + k] - means[k]) / (2.0 * (means[2 + k] + EPSILON)))
        for k in range(2)
    ]
    wave_y = signed_row((1, N)).astype(F32) * WAVE
    start = lanes((64, 128)) == 0
    for x in range(4):
        for f in range(FIELDS_BACK):
            near, far = (
                came[pl.ds(f * 8 + low * 4 + x, 128, stride=ROWS_BACK), :] for low in range(2)
            )
            even, odd = (near + far).T, (near - far).T
            real, imag = odd[:64], odd[64:]
            turned = (jnp.where(start, real, imag), jnp.where(start, imag, -real))
            rows = slice((x * FIELDS_BACK + f) * 128, (x * FIELDS_BACK + f + 1) * 128)
            left_high[rows, :128], left_low[rows, :128] = split(even)
            left_high[rows, 128:], left_low[rows, 128:] = split(jnp.concatenate(turned, axis=0))
        rows = slice(x * FIELDS_BACK * 128, (x + 1) * FIELDS_BACK * 128)
        got[rows] = product(
            (left_high[rows], left_low[rows]), (yf_high[...], yf_low[...]), ((1,), (0,))
        )

    copies = []
    for block in range(64 // BLOCK):
        low = block * BLOCK
        grow = grown[low // GMODES]
        wave_z = factors[6, 0, low : low + BLOCK]
        for x in range(4):
            wave_x = (slab * 4 + x).astype(F32) * WAVE
            main, turn, slow, lift, inverse_sq, step = (
                factors[k, x, low : low + BLOCK] for k in range(6)
            )

            def part(f, k):
                row = (x * FIELDS_BACK + f) * 128 + k * 64 + low
                return got[row : row + BLOCK]

            for k in range(2):
                source = part(3, 1 - k) + wave_y * part(4, 1 - k)
                flows = [
                    jnp.concatenate(
                        [
                            state[f * 2 + k, pl.ds(low * 8 + h * 4 + x, BLOCK, stride=8), :]
                            for h in range(2)
                        ],
                        axis=1,
                    )
                    for f in range(4)
                ]
                right = [flows[f] * grow + step * part(f, k) for f in range(3)]
                right_b = flows[3] + (step * source if k == 0 else -(step * source))
                new_x = main * right[0] + turn * right[1]
                new_y = main * right[1] - turn * right[0]
                new_z = slow * right[2] + lift * right_b
                new_b = slow * right_b - BRUNT_SQUARED * (lift * right[2])
                inner = (wave_x * new_x + wave_y * new_y + wave_z * new_z) * inverse_sq
                made = (
                    new_x - wave_x * inner,
                    new_y - wave_y * inner,
                    new_z - wave_z * inner,
                    new_b,
                )
                for f in range(4):
                    for h in range(2):
                        rows = pl.ds(low * 8 + h * 4 + x, BLOCK, stride=8)
                        made_state[f * 2 + k, rows, :] = made[f][:, h * 128 : (h + 1) * 128]
        if block % 2:
            rows = pl.ds((block - 1) * BLOCK * 8, 2 * BLOCK * 8)
            copy = pltpu.make_async_copy(
                made_state.at[:, rows], made_far.at[:, rows], sems.at[block // 2]
            )
            copy.start()
            copies.append(copy)
    for copy in copies:
        copy.wait()


VM = pl.BlockSpec(memory_space=pltpu.VMEM)
SM = pl.BlockSpec(memory_space=pltpu.SMEM)
HBM = pl.BlockSpec(memory_space=pltpu.HBM)


def far(array):
    return pltpu.with_memory_space_constraint(array, pltpu.HBM)


def granted(mebibytes):
    return pltpu.CompilerParams(vmem_limit_bytes=mebibytes << 20)


def shards(state, kz_group, cutoffs, damping, power):
    y_inverse, z_table, x_inverse, x_forward, y_forward = tables()
    groups = kz_group.reshape(1, N)
    rows = state.reshape(4, 2, 64, 4, 2, 128).transpose(0, 1, 2, 4, 3, 5).reshape(8, 512, 128)

    sent, sums, factors = pl.pallas_call(
        send_kernel,
        out_shape=(
            jax.ShapeDtypeStruct((128 * ROWS_OUT, 128), F32),
            jax.ShapeDtypeStruct((8, 128), F32),
            jax.ShapeDtypeStruct((7, 4, 64, N), F32),
        ),
        in_specs=[HBM] * 6,
        out_specs=(VM, VM, VM),
        scratch_shapes=[
            pltpu.SMEM((3,), jnp.int32),
            pltpu.SMEM((GROUPS,), F32),
            pltpu.VMEM((1, N), jnp.int32),
            pltpu.VMEM((8, 512, 128), F32),
            pltpu.VMEM((512, N), BF16),
            pltpu.VMEM((512, N), BF16),
            pltpu.SemaphoreType.DMA((11,)),
        ],
        compiler_params=granted(SEND_MIB),
        name="send",
    )(*(far(a) for a in (cutoffs, damping, groups, rows, *y_inverse)))
    came = lax.all_to_all(sent.reshape(128, ROWS_OUT, 128), ALL, 0, 0, tiled=True)

    back = pl.pallas_call(
        grid_kernel,
        out_shape=jax.ShapeDtypeStruct((128 * ROWS_BACK, 128), F32),
        in_specs=[VM] * 9,
        out_specs=VM,
        scratch_shapes=[
            pltpu.VMEM((N, N), BF16),
            pltpu.VMEM((N, N), BF16),
            pltpu.VMEM((7, 256, 512), F32),
            pltpu.VMEM((7, 256, 512), F32),
            pltpu.VMEM((6, 4 * KEPT_COLS, N), F32),
        ],
        compiler_params=granted(GRID_MIB),
        name="grid",
    )(came, sums, groups, *z_table, *x_inverse, *x_forward)
    came = lax.all_to_all(back.reshape(128, 1, ROWS_BACK * 128), ALL, 0, 0, tiled=True)

    made = pl.pallas_call(
        update_kernel,
        out_shape=jax.ShapeDtypeStruct((8, 512, 128), F32),
        in_specs=[SM] + [VM] * 5,
        out_specs=HBM,
        scratch_shapes=[
            pltpu.VMEM((20 * 128, N), BF16),
            pltpu.VMEM((20 * 128, N), BF16),
            pltpu.VMEM((20 * 128, N), F32),
            pltpu.VMEM((8, 512, 128), F32),
            pltpu.SemaphoreType.DMA((32 // BLOCK,)),
        ],
        compiler_params=granted(UPDATE_MIB),
        name="update",
    )(power, came.reshape(128 * ROWS_BACK, 128), rows, factors, *y_forward)
    made = made.reshape(4, 2, 64, 2, 4, 128).transpose(0, 1, 2, 4, 3, 5)
    return made.reshape(4, 2, 64, 4, N)


def solution(mesh):
    finer = Mesh(
        mesh.devices.reshape(mesh.shape["grp"], 4, 4, 2), ("grp", "slab_0", "slab_1", "slab_2")
    )
    return jax.shard_map(
        shards,
        mesh=finer,
        in_specs=(P(None, None, "grp", SLAB, None), P(), P(), P(), P()),
        out_specs=P(None, None, "grp", SLAB, None),
        check_vma=False,
    )
```

```python
import functools
import math

import jax
import jax.numpy as jnp
import numpy as np
from jax import lax
from jax.experimental import pallas as pl
from jax.experimental.pallas import tpu as pltpu
from jax.sharding import Mesh
from jax.sharding import PartitionSpec as P

N = 256
GROUPS = 8
KX = 128
GMODES = 32
KEPT_COLS = 88
SLAB = ("slab_0", "slab_1", "slab_2")
ALL = ("grp",) + SLAB
HALF = N // 2

TWO_PI = 6.283185307179586
WAVE = TWO_PI / N
TIME_STEP = 0.25
CORIOLIS = 1.0
BRUNT_SQUARED = 2.0
EPSILON = 1e-06
SCALE = 1.0 / 4096.0
FIELDS_OUT = 6
FIELDS_BACK = 5
ROWS_OUT = 8 * FIELDS_OUT
ROWS_BACK = 8 * FIELDS_BACK + 1

SEND_MIB = 24
GRID_MIB = 40
UPDATE_MIB = 28

F32 = jnp.float32
BF16 = jnp.bfloat16


def halves(table):
    high = table.astype(np.float32).astype(jnp.bfloat16)
    low = (table - high.astype(np.float64)).astype(np.float32).astype(jnp.bfloat16)
    return jnp.asarray(high), jnp.asarray(low)


def angle(rows, cols):
    return 2.0 * np.pi / N * (np.outer(rows, cols) % N).astype(np.float64)


def signed(index):
    return np.where(index < N // 2, index, index - N)


def folded():
    theta = angle(np.arange(HALF), np.arange(N))
    cosine, sine = np.cos(theta), np.sin(theta)
    odd = np.arange(N) % 2
    cosine[0], sine[0] = 1 - odd, odd
    return np.stack([cosine, sine])


def tables():
    points = np.arange(N)
    pair = folded()
    wave = (WAVE * signed(points))[None, None, :]
    y_inverse = np.concatenate([pair, wave * pair]).reshape(4 * HALF, N)
    fold = pair.reshape(N, N)
    theta = angle(points, np.arange(KX))
    weight = np.where(np.arange(KX) == 0, 1.0, 2.0) * SCALE
    x_inverse = np.concatenate([np.cos(theta) * weight, -np.sin(theta) * weight], axis=1)
    theta = theta.T[:KEPT_COLS]
    x_forward = np.concatenate([np.cos(theta), -np.sin(theta)], axis=0) * SCALE
    return [halves(t) for t in (y_inverse, fold.T.copy(), x_inverse, x_forward, fold)]


def split(value):
    high = value.astype(BF16)
    low = (value - high.astype(F32)).astype(BF16)
    return high, low


def product(left, right, dims):
    def one(a, b):
        return lax.dot_general(a, b, (dims, ((), ())), preferred_element_type=F32)

    return one(left[0], right[0]) + (one(left[0], right[1]) + one(left[1], right[0]))


def slot_rows(group_row, slots):
    member = (lax.broadcasted_iota(jnp.int32, (GROUPS, N), 0) == group_row).astype(F32)
    earlier = (
        lax.broadcasted_iota(jnp.int32, (N, N), 0) < lax.broadcasted_iota(jnp.int32, (N, N), 1)
    ).astype(F32)
    count = jnp.dot(member.astype(BF16), earlier.astype(BF16), preferred_element_type=F32)
    first = (GMODES * lax.broadcasted_iota(jnp.int32, (GROUPS, N), 0)).astype(F32)
    place = jnp.sum(member * (first + count), axis=0, keepdims=True).astype(jnp.int32)
    return slots == place


def signed_row(shape):
    index = lax.broadcasted_iota(jnp.int32, shape, len(shape) - 1)
    return jnp.where(index < N // 2, index, index - N)


def lanes(shape):
    return lax.broadcasted_iota(jnp.int32, shape, len(shape) - 1)


def fill_factors(cutoffs, damping_of, power_of, groups, factors):
    grp = lax.axis_index("grp")
    slab = lax.axis_index(SLAB)
    here = slot_rows(groups[...], lax.broadcasted_iota(jnp.int32, (64, N), 0) + grp * 64)
    mode_z = jnp.sum(jnp.where(here, signed_row((64, N)), 0), axis=1, keepdims=True)
    mode_y = signed_row((1, N))
    slot = lax.broadcasted_iota(jnp.int32, (64, 1), 0)
    damping = jnp.where(slot < GMODES, damping_of[grp * 2], damping_of[grp * 2 + 1])
    wave_z = mode_z.astype(F32) * WAVE
    wave_y = mode_y.astype(F32) * WAVE
    kept_zy = (96 * jnp.abs(mode_z) <= cutoffs[2] * N) & (96 * jnp.abs(mode_y) <= cutoffs[1] * N)
    wave_zy = wave_y * wave_y + wave_z * wave_z
    rotation = TIME_STEP * CORIOLIS
    for x in range(4):
        mode_x = slab * 4 + x
        wave_x = mode_x.astype(F32) * WAVE
        kept = kept_zy & (96 * mode_x <= cutoffs[0] * N)
        wave_sq = wave_x * wave_x + wave_zy
        implicit = 1.0 + TIME_STEP * damping * wave_sq
        square = implicit * implicit
        first = 1.0 / (square + rotation * rotation)
        second = 1.0 / (square + TIME_STEP * TIME_STEP * BRUNT_SQUARED)
        factors[0, x] = implicit * first
        factors[1, x] = rotation * first
        factors[2, x] = implicit * second
        factors[3, x] = TIME_STEP * second
        factors[4, x] = 1.0 / jnp.where(wave_sq == 0, 1.0, wave_sq)
        factors[5, x] = jnp.where(kept, TIME_STEP, 0.0)
    factors[6, 0] = jnp.broadcast_to(wave_z, (64, N))
    power = jnp.where(slot < GMODES, power_of[grp * 2], power_of[grp * 2 + 1])
    factors[6, 1] = jnp.broadcast_to(power, (64, N))


def send_kernel(
    cutoffs_far,
    damping_far,
    power_far,
    groups_far,
    state_far,
    w_high_far,
    w_low_far,
    sent,
    sums,
    factors,
    cutoffs,
    damping_of,
    power_of,
    groups,
    state,
    w_high,
    w_low,
    sems,
):
    copies = {}

    def fetch(key, source, target, k):
        copies[key] = pltpu.make_async_copy(source, target, sems.at[k])
        copies[key].start()

    small = (
        (groups_far, groups),
        (cutoffs_far, cutoffs),
        (damping_far, damping_of),
        (power_far, power_of),
    )
    for k, (source, target) in enumerate(small):
        fetch(k, source, target, 8 + k)
    order = (1, 0, 2, 3)
    for k, low in enumerate((0, N)):
        rows = pl.ds(low, N)
        if k == 0:
            fetch("high0", w_high_far.at[rows], w_high.at[rows], 0)
            fetch("state1", state_far.at[pl.ds(2, 2)], state.at[pl.ds(2, 2)], 1)
            fetch("low0", w_low_far.at[rows], w_low.at[rows], 2)
        else:
            fetch("high1", w_high_far.at[rows], w_high.at[rows], 3)
            fetch("low1", w_low_far.at[rows], w_low.at[rows], 4)
    for k, f in enumerate(order[1:]):
        rows = pl.ds(2 * f, 2)
        fetch("state" + str(f), state_far.at[rows], state.at[rows], 5 + k)

    for k in range(4):
        copies[k].wait()
    fill_factors(cutoffs, damping_of, power_of, groups, factors)

    sign = jnp.where(lanes((HALF, 128)) < 64, -1.0, 1.0).astype(F32)
    top = lax.broadcasted_iota(jnp.int32, (HALF, 128), 0) == 0
    flux = jnp.zeros((128, N), F32)
    energy = jnp.zeros((128, N), F32)

    def put(slot, x, even, odd):
        for low, value in ((0, even + odd), (1, even - odd)):
            sent[pl.ds(slot * 8 + low * 4 + x, 128, stride=ROWS_OUT), :] = value

    def piece(f, pair):
        rows = []
        for x in (2 * pair, 2 * pair + 1):
            for part in range(2):
                rows.append(
                    jnp.concatenate(
                        [state[f * 2 + part, pl.ds(h * 4 + x, 64, stride=8), :] for h in range(2)],
                        axis=1,
                    )
                )
        return jnp.concatenate(rows, axis=0)

    for f in order:
        if f == 1:
            for key in ("high0", "low0", "high1", "low1", "state1", "state0"):
                copies[key].wait()
        if f == 2:
            copies["state2"].wait()
            copies["state3"].wait()
        derived = {0: 4, 2: 5}.get(f)
        count = 512 if derived else 256
        share = 0.5 / BRUNT_SQUARED if f == 3 else 0.5
        for pair in range(2):
            value = piece(f, pair)
            square = share * (value * value)
            energy = energy + (square[:128] + square[128:])
            if f == 3:
                moved = value * piece(2, pair)
                flux = flux + (moved[:128] + moved[128:])
            made = product((w_high[:count], w_low[:count]), split(value), ((1,), (1,)))
            for k in range(2):
                x = pair * 2 + k
                cols = slice(k * 128, (k + 1) * 128)
                even, odd = made[0:128, cols], made[128:256, cols]
                put(f, x, even, jnp.where(top, odd, sign * pltpu.roll(odd, 64, 1)))
                if derived:
                    even, odd = made[256:384, cols], made[384:512, cols]
                    even = sign * pltpu.roll(even, 64, 1)
                    put(derived, x, even, jnp.where(top, sign * pltpu.roll(odd, 64, 1), -odd))

    quarter = lanes((1, 128)) // 32
    total = jnp.zeros((1, 128), F32)
    for k, value in enumerate((flux, energy)):
        for which in range(2):
            low = which * GMODES
            part = jnp.sum(value[low : low + 32] + value[64 + low : 96 + low], axis=0, keepdims=True)
            part = part[:, :128] + part[:, 128:]
            part = part + pltpu.roll(part, 64, 1)
            part = part + pltpu.roll(part, 32, 1)
            total = jnp.where(quarter == 2 * k + which, part, total)
    sums[...] = jnp.broadcast_to(total, (8, 128))


def grid_kernel(
    came,
    sums,
    groups,
    zt_high,
    zt_low,
    xi_high,
    xi_low,
    xf_high,
    xf_low,
    sent,
    wz_high,
    wz_low,
    rows_z,
    planes,
    lines,
):
    picked = slot_rows(groups[...], lax.broadcasted_iota(jnp.int32, (N, N), 0)).astype(BF16)
    for table, out in ((zt_high, wz_high), (zt_low, wz_low)):
        out[...] = jnp.dot(picked, table[...], preferred_element_type=F32).astype(BF16)
    kz = lax.dot_general(
        signed_row((8, N)).astype(F32).astype(BF16),
        picked,
        (((1,), (1,)), ((), ())),
        preferred_element_type=F32,
    )
    kz = kz[0:1, :] * WAVE
    kx = (lax.broadcasted_iota(jnp.int32, (N, 1), 0) % 128).astype(F32) * WAVE
    weights = (wz_high[...], wz_low[...])

    def separate(first, second):
        low = lanes(first.shape) < 64
        return (
            jnp.where(low, first, pltpu.roll(second, 64, 1)),
            jnp.where(low, pltpu.roll(first, 64, 1), second),
        )

    upper = lax.broadcasted_iota(jnp.int32, (16, 8, 128), 1) < 4

    def field(f):
        pieces = []
        for g in range(4):
            tiles = came[g * 32 : (g + 1) * 32, f * 8 : (f + 1) * 8, :].reshape(16, 2, 8, 128)
            even, odd = tiles[:, 0], tiles[:, 1]
            first = jnp.where(upper, even, pltpu.roll(odd, 4, 1))
            second = jnp.where(upper, pltpu.roll(even, 4, 1), odd)
            pieces.append(
                jnp.concatenate([first.reshape(128, 128), second.reshape(128, 128)], axis=0)
            )
        near, far = separate(pieces[0], pieces[1]), separate(pieces[2], pieces[3])
        return tuple(jnp.concatenate([near[k], far[k]], axis=1) for k in range(2))

    start = lanes((N, HALF)) == 0

    def vertical(value, slot):
        made = product(split(jnp.concatenate(value, axis=0)), weights, ((1,), (0,)))
        even = (made[:N, :HALF], made[N:, :HALF])
        odd = (made[:N, HALF:], made[N:, HALF:])
        turned = (jnp.where(start, odd[0], -odd[1]), jnp.where(start, odd[1], odd[0]))
        for part in range(2):
            for k, both in enumerate((even[part] + turned[part], even[part] - turned[part])):
                for plane in range(2):
                    col = plane * N + k * HALF
                    rows_z[slot, part * 128 : (part + 1) * 128, col : col + HALF] = both[
                        plane * 128 : (plane + 1) * 128
                    ]

    flow_x = field(0)
    vertical(flow_x, 0)
    flow_z = field(2)
    vertical(flow_z, 2)
    vertical(
        (kx * flow_z[1] - kz * flow_x[1], kz * flow_x[0] - kx * flow_z[0]),
        5,
    )
    flow_y = field(1)
    vertical(flow_y, 1)
    slope = field(5)
    vertical((slope[0] + kz * flow_y[1], slope[1] - kz * flow_y[0]), 4)
    slope = field(4)
    vertical((-(kx * flow_y[1]) - slope[0], kx * flow_y[0] - slope[1]), 6)
    vertical(field(3), 3)

    x_inverse = (xi_high[...], xi_low[...])
    for slot in range(7):
        planes[slot] = product(x_inverse, split(rows_z[slot]), ((1,), (0,)))

    x_forward = (xf_high[...], xf_low[...])
    start_kept = lanes((KEPT_COLS, HALF)) == 0

    def horizontal(value, slot):
        pieces = []
        for plane in range(2):
            near = value[:, plane * N : plane * N + HALF]
            far = value[:, plane * N + HALF : (plane + 1) * N]
            pieces += [near + far, near - far]
        made = product(x_forward, split(jnp.concatenate(pieces, axis=1)), ((1,), (0,)))
        for plane in range(2):
            col = plane * N
            plus = made[:, col : col + HALF]
            odd_real = made[:KEPT_COLS, col + HALF : col + N]
            odd_imag = made[KEPT_COLS:, col + HALF : col + N]
            real, imag = plane * KEPT_COLS, (2 + plane) * KEPT_COLS
            lines[slot, real : real + KEPT_COLS, :HALF] = plus[:KEPT_COLS]
            lines[slot, imag : imag + KEPT_COLS, :HALF] = plus[KEPT_COLS:]
            lines[slot, real : real + KEPT_COLS, HALF:] = jnp.where(start_kept, odd_real, odd_imag)
            lines[slot, imag : imag + KEPT_COLS, HALF:] = jnp.where(
                start_kept, odd_imag, -odd_real
            )

    u, v, w, b, ox, oy, oz = range(7)
    horizontal(planes[v] * planes[oz] - planes[w] * planes[oy], 0)
    horizontal(planes[w] * planes[ox] - planes[u] * planes[oz], 1)
    horizontal(planes[u] * planes[oy] - planes[v] * planes[ox], 2)
    horizontal(planes[u] * planes[b], 3)
    horizontal(planes[v] * planes[b], 4)
    horizontal(planes[w] * planes[b], 5)

    row = lax.broadcasted_iota(jnp.int32, (4 * KEPT_COLS, 1), 0)
    kx_kept = (row % KEPT_COLS).astype(F32) * WAVE
    upper_kept = lax.broadcasted_iota(jnp.int32, (11, 8, 128), 1) < 4

    def slots(value):
        return product(split(value), weights, ((1,), (1,)))

    for g in range(4):
        low = (g * 32 + 22) * ROWS_BACK
        sent[low : low + 10 * ROWS_BACK] = jnp.zeros((10 * ROWS_BACK, 128), F32)

    def put(value, f):
        for pair in range(2):
            cols = slice(pair * 128, (pair + 1) * 128)
            both = separate(value[: 2 * KEPT_COLS, cols], value[2 * KEPT_COLS :, cols])
            for k in range(2):
                g = 2 * pair + k
                first = both[k][:KEPT_COLS].reshape(11, 8, 128)
                second = both[k][KEPT_COLS:].reshape(11, 8, 128)
                even = jnp.where(upper_kept, first, pltpu.roll(second, 4, 1))
                odd = jnp.where(upper_kept, pltpu.roll(first, 4, 1), second)
                for j in range(11):
                    low = (g * 32 + 2 * j) * ROWS_BACK + f * 8
                    sent[low : low + 8, :] = even[j]
                    sent[low + ROWS_BACK : low + ROWS_BACK + 8, :] = odd[j]

    for k in range(3):
        put(slots(lines[k]), k)
    put(kx_kept * slots(lines[3]) + kz * slots(lines[5]), 3)
    put(slots(lines[4]), 4)
    sent[pl.ds(8 * FIELDS_BACK, 128, stride=ROWS_BACK), :] = jnp.broadcast_to(
        sums[0:1, :], (128, 128)
    )


BLOCK = 8


def update_kernel(
    came, state, factors, yf_high, yf_low, made_far, left_high, left_low, got, made_state, sems
):
    grp = lax.axis_index("grp")
    slab = lax.axis_index(SLAB)
    source_grp = lax.broadcasted_iota(jnp.int32, (128, 128), 0) // 32
    total = came[pl.ds(8 * FIELDS_BACK, 128, stride=ROWS_BACK), :]
    total = jnp.sum(jnp.where(source_grp == grp, total, 0.0), axis=0, keepdims=True)
    quarter = lanes((1, 128)) // 32
    means = [
        jnp.sum(jnp.where(quarter == k, total, 0.0), axis=1, keepdims=True) / (GMODES * KX * N)
        for k in range(4)
    ]
    wave_y = signed_row((1, N)).astype(F32) * WAVE
    start = lanes((64, 128)) == 0
    for x in range(4):
        for f in range(FIELDS_BACK):
            near, far = (
                came[pl.ds(f * 8 + low * 4 + x, 128, stride=ROWS_BACK), :] for low in range(2)
            )
            even, odd = (near + far).T, (near - far).T
            real, imag = odd[:64], odd[64:]
            turned = (jnp.where(start, real, imag), jnp.where(start, imag, -real))
            rows = slice((x * FIELDS_BACK + f) * 128, (x * FIELDS_BACK + f + 1) * 128)
            left_high[rows, :128], left_low[rows, :128] = split(even)
            left_high[rows, 128:], left_low[rows, 128:] = split(jnp.concatenate(turned, axis=0))
        rows = slice(x * FIELDS_BACK * 128, (x + 1) * FIELDS_BACK * 128)
        got[rows] = product(
            (left_high[rows], left_low[rows]), (yf_high[...], yf_low[...]), ((1,), (0,))
        )

    blocks = 64 // BLOCK

    def out_copy(block):
        rows = pl.ds(pl.multiple_of(block * (8 * BLOCK), 8 * BLOCK), 8 * BLOCK)
        return pltpu.make_async_copy(
            made_state.at[:, rows], made_far.at[:, rows], sems.at[block]
        )

    def step_block(block, carry):
        low = pl.multiple_of(block * BLOCK, BLOCK)
        high = block * BLOCK >= GMODES
        flux = jnp.where(high, means[1], means[0])
        energy = jnp.where(high, means[3], means[2])
        wave_z = factors[6, 0, pl.ds(low, BLOCK)]
        power = factors[6, 1, pl.ds(low, BLOCK)]
        grow = 1.0 + TIME_STEP * ((power - flux) / (2.0 * (energy + EPSILON)))
        for x in range(4):
            wave_x = (slab * 4 + x).astype(F32) * WAVE
            main, turn, slow, lift, inverse_sq, step = (
                factors[k, x, pl.ds(low, BLOCK)] for k in range(6)
            )

            def part(f, k):
                return got[pl.ds((x * FIELDS_BACK + f) * 128 + k * 64 + low, BLOCK)]

            for k in range(2):
                source = part(3, 1 - k) + wave_y * part(4, 1 - k)
                flows = [
                    jnp.concatenate(
                        [
                            state[f * 2 + k, pl.ds(low * 8 + h * 4 + x, BLOCK, stride=8), :]
                            for h in range(2)
                        ],
                        axis=1,
                    )
                    for f in range(4)
                ]
                right = [flows[f] * grow + step * part(f, k) for f in range(3)]
                right_b = flows[3] + (step * source if k == 0 else -(step * source))
                new_x = main * right[0] + turn * right[1]
                new_y = main * right[1] - turn * right[0]
                new_z = slow * right[2] + lift * right_b
                new_b = slow * right_b - BRUNT_SQUARED * (lift * right[2])
                inner = (wave_x * new_x + wave_y * new_y + wave_z * new_z) * inverse_sq
                made = (
                    new_x - wave_x * inner,
                    new_y - wave_y * inner,
                    new_z - wave_z * inner,
                    new_b,
                )
                for f in range(4):
                    for h in range(2):
                        rows = pl.ds(low * 8 + h * 4 + x, BLOCK, stride=8)
                        made_state[f * 2 + k, rows, :] = made[f][:, h * 128 : (h + 1) * 128]
        out_copy(block).start()
        return carry

    lax.fori_loop(0, blocks, step_block, 0)
    for block in range(blocks):
        out_copy(block).wait()


VM = pl.BlockSpec(memory_space=pltpu.VMEM)
HBM = pl.BlockSpec(memory_space=pltpu.HBM)


def far(array):
    return pltpu.with_memory_space_constraint(array, pltpu.HBM)


def granted(mebibytes):
    return pltpu.CompilerParams(vmem_limit_bytes=mebibytes << 20)


def shards(state, kz_group, cutoffs, damping, power):
    y_inverse, z_table, x_inverse, x_forward, y_forward = tables()
    groups = kz_group.reshape(1, N)
    rows = state.reshape(4, 2, 64, 4, 2, 128).transpose(0, 1, 2, 4, 3, 5).reshape(8, 512, 128)

    sent, sums, factors = pl.pallas_call(
        send_kernel,
        out_shape=(
            jax.ShapeDtypeStruct((128 * ROWS_OUT, 128), F32),
            jax.ShapeDtypeStruct((8, 128), F32),
            jax.ShapeDtypeStruct((7, 4, 64, N), F32),
        ),
        in_specs=[HBM] * 7,
        out_specs=(VM, VM, VM),
        scratch_shapes=[
            pltpu.SMEM((3,), jnp.int32),
            pltpu.SMEM((GROUPS,), F32),
            pltpu.SMEM((GROUPS,), F32),
            pltpu.VMEM((1, N), jnp.int32),
            pltpu.VMEM((8, 512, 128), F32),
            pltpu.VMEM((512, N), BF16),
            pltpu.VMEM((512, N), BF16),
            pltpu.SemaphoreType.DMA((12,)),
        ],
        compiler_params=granted(SEND_MIB),
        name="send",
    )(*(far(a) for a in (cutoffs, damping, power, groups, rows, *y_inverse)))
    came = lax.all_to_all(sent.reshape(128, ROWS_OUT, 128), ALL, 0, 0, tiled=True)

    back = pl.pallas_call(
        grid_kernel,
        out_shape=jax.ShapeDtypeStruct((128 * ROWS_BACK, 128), F32),
        in_specs=[VM] * 9,
        out_specs=VM,
        scratch_shapes=[
            pltpu.VMEM((N, N), BF16),
            pltpu.VMEM((N, N), BF16),
            pltpu.VMEM((7, 256, 512), F32),
            pltpu.VMEM((7, 256, 512), F32),
            pltpu.VMEM((6, 4 * KEPT_COLS, N), F32),
        ],
        compiler_params=granted(GRID_MIB),
        name="grid",
    )(came, sums, groups, *z_table, *x_inverse, *x_forward)
    came = lax.all_to_all(back.reshape(128, 1, ROWS_BACK * 128), ALL, 0, 0, tiled=True)

    made = pl.pallas_call(
        update_kernel,
        out_shape=jax.ShapeDtypeStruct((8, 512, 128), F32),
        in_specs=[VM] * 5,
        out_specs=HBM,
        scratch_shapes=[
            pltpu.VMEM((20 * 128, N), BF16),
            pltpu.VMEM((20 * 128, N), BF16),
            pltpu.VMEM((20 * 128, N), F32),
            pltpu.VMEM((8, 512, 128), F32),
            pltpu.SemaphoreType.DMA((64 // BLOCK,)),
        ],
        compiler_params=granted(UPDATE_MIB),
        name="update",
    )(came.reshape(128 * ROWS_BACK, 128), rows, factors, *y_forward)
    made = made.reshape(4, 2, 64, 2, 4, 128).transpose(0, 1, 2, 4, 3, 5)
    return made.reshape(4, 2, 64, 4, N)


def solution(mesh):
    finer = Mesh(
        mesh.devices.reshape(mesh.shape["grp"], 4, 4, 2), ("grp", "slab_0", "slab_1", "slab_2")
    )
    return jax.shard_map(
        shards,
        mesh=finer,
        in_specs=(P(None, None, "grp", SLAB, None), P(), P(), P(), P()),
        out_specs=P(None, None, "grp", SLAB, None),
        check_vma=False,
    )
```

```python
import functools
import math

import jax
import jax.numpy as jnp
import numpy as np
from jax import lax
from jax.experimental import pallas as pl
from jax.experimental.pallas import tpu as pltpu
from jax.sharding import Mesh
from jax.sharding import PartitionSpec as P

N = 256
GROUPS = 8
KX = 128
GMODES = 32
KEPT_COLS = 88
SLAB = ("slab_0", "slab_1", "slab_2")
ALL = ("grp",) + SLAB
HALF = N // 2

TWO_PI = 6.283185307179586
WAVE = TWO_PI / N
TIME_STEP = 0.25
CORIOLIS = 1.0
BRUNT_SQUARED = 2.0
EPSILON = 1e-06
SCALE = 1.0 / 4096.0
FIELDS_OUT = 6
FIELDS_BACK = 5
ROWS_OUT = 8 * FIELDS_OUT + 1
ROWS_BACK = 8 * FIELDS_BACK

SEND_MIB = 24
GRID_MIB = 40
UPDATE_MIB = 28

F32 = jnp.float32
BF16 = jnp.bfloat16


def halves(table):
    high = table.astype(np.float32).astype(jnp.bfloat16)
    low = (table - high.astype(np.float64)).astype(np.float32).astype(jnp.bfloat16)
    return jnp.asarray(high), jnp.asarray(low)


def angle(rows, cols):
    return 2.0 * np.pi / N * (np.outer(rows, cols) % N).astype(np.float64)


def signed(index):
    return np.where(index < N // 2, index, index - N)


def folded():
    theta = angle(np.arange(HALF), np.arange(N))
    cosine, sine = np.cos(theta), np.sin(theta)
    odd = np.arange(N) % 2
    cosine[0], sine[0] = 1 - odd, odd
    return np.stack([cosine, sine])


def tables():
    points = np.arange(N)
    pair = folded()
    wave = (WAVE * signed(points))[None, None, :]
    y_inverse = np.concatenate([pair, wave * pair]).reshape(4 * HALF, N)
    fold = pair.reshape(N, N)
    theta = angle(points, np.arange(KX))
    weight = np.where(np.arange(KX) == 0, 1.0, 2.0) * SCALE
    x_inverse = np.concatenate([np.cos(theta) * weight, -np.sin(theta) * weight], axis=1)
    theta = theta.T[:KEPT_COLS]
    x_forward = np.concatenate([np.cos(theta), -np.sin(theta)], axis=0) * SCALE
    return [halves(t) for t in (y_inverse, fold.T.copy(), x_inverse, x_forward, fold)]


def split(value):
    high = value.astype(BF16)
    low = (value - high.astype(F32)).astype(BF16)
    return high, low


def product(left, right, dims):
    def one(a, b):
        return lax.dot_general(a, b, (dims, ((), ())), preferred_element_type=F32)

    return one(left[0], right[0]) + (one(left[0], right[1]) + one(left[1], right[0]))


def slot_rows(group_row, slots):
    member = (lax.broadcasted_iota(jnp.int32, (GROUPS, N), 0) == group_row).astype(F32)
    earlier = (
        lax.broadcasted_iota(jnp.int32, (N, N), 0) < lax.broadcasted_iota(jnp.int32, (N, N), 1)
    ).astype(F32)
    count = jnp.dot(member.astype(BF16), earlier.astype(BF16), preferred_element_type=F32)
    first = (GMODES * lax.broadcasted_iota(jnp.int32, (GROUPS, N), 0)).astype(F32)
    place = jnp.sum(member * (first + count), axis=0, keepdims=True).astype(jnp.int32)
    return slots == place


def signed_row(shape):
    index = lax.broadcasted_iota(jnp.int32, shape, len(shape) - 1)
    return jnp.where(index < N // 2, index, index - N)


def lanes(shape):
    return lax.broadcasted_iota(jnp.int32, shape, len(shape) - 1)


def fill_factors(cutoffs, damping_of, power_of, groups, factors):
    grp = lax.axis_index("grp")
    slab = lax.axis_index(SLAB)
    here = slot_rows(groups[...], lax.broadcasted_iota(jnp.int32, (64, N), 0) + grp * 64)
    mode_z = jnp.sum(jnp.where(here, signed_row((64, N)), 0), axis=1, keepdims=True)
    mode_y = signed_row((1, N))
    slot = lax.broadcasted_iota(jnp.int32, (64, 1), 0)
    damping = jnp.where(slot < GMODES, damping_of[grp * 2], damping_of[grp * 2 + 1])
    wave_z = mode_z.astype(F32) * WAVE
    wave_y = mode_y.astype(F32) * WAVE
    kept_zy = (96 * jnp.abs(mode_z) <= cutoffs[2] * N) & (96 * jnp.abs(mode_y) <= cutoffs[1] * N)
    wave_zy = wave_y * wave_y + wave_z * wave_z
    rotation = TIME_STEP * CORIOLIS
    for x in range(4):
        mode_x = slab * 4 + x
        wave_x = mode_x.astype(F32) * WAVE
        kept = kept_zy & (96 * mode_x <= cutoffs[0] * N)
        wave_sq = wave_x * wave_x + wave_zy
        implicit = 1.0 + TIME_STEP * damping * wave_sq
        square = implicit * implicit
        first = 1.0 / (square + rotation * rotation)
        second = 1.0 / (square + TIME_STEP * TIME_STEP * BRUNT_SQUARED)
        factors[0, x] = implicit * first
        factors[1, x] = rotation * first
        factors[2, x] = implicit * second
        factors[3, x] = TIME_STEP * second
        factors[4, x] = 1.0 / jnp.where(wave_sq == 0, 1.0, wave_sq)
        factors[5, x] = jnp.where(kept, TIME_STEP, 0.0)
    factors[6, 0] = jnp.broadcast_to(wave_z, (64, N))
    power = jnp.where(slot < GMODES, power_of[grp * 2], power_of[grp * 2 + 1])
    factors[6, 1] = jnp.broadcast_to(power, (64, N))


def send_kernel(
    cutoffs_far,
    damping_far,
    power_far,
    groups_far,
    state_far,
    w_high_far,
    w_low_far,
    sent,
    factors,
    cutoffs,
    damping_of,
    power_of,
    groups,
    state,
    w_high,
    w_low,
    sems,
):
    copies = {}

    def fetch(key, source, target, k):
        copies[key] = pltpu.make_async_copy(source, target, sems.at[k])
        copies[key].start()

    small = (
        (groups_far, groups),
        (cutoffs_far, cutoffs),
        (damping_far, damping_of),
        (power_far, power_of),
    )
    for k, (source, target) in enumerate(small):
        fetch(k, source, target, 8 + k)
    order = (1, 0, 2, 3)
    for k, low in enumerate((0, N)):
        rows = pl.ds(low, N)
        if k == 0:
            fetch("high0", w_high_far.at[rows], w_high.at[rows], 0)
            fetch("state1", state_far.at[pl.ds(2, 2)], state.at[pl.ds(2, 2)], 1)
            fetch("low0", w_low_far.at[rows], w_low.at[rows], 2)
        else:
            fetch("high1", w_high_far.at[rows], w_high.at[rows], 3)
            fetch("low1", w_low_far.at[rows], w_low.at[rows], 4)
    for k, f in enumerate(order[1:]):
        rows = pl.ds(2 * f, 2)
        fetch("state" + str(f), state_far.at[rows], state.at[rows], 5 + k)

    for k in range(4):
        copies[k].wait()
    fill_factors(cutoffs, damping_of, power_of, groups, factors)

    sign = jnp.where(lanes((HALF, 128)) < 64, -1.0, 1.0).astype(F32)
    top = lax.broadcasted_iota(jnp.int32, (HALF, 128), 0) == 0
    flux = jnp.zeros((128, N), F32)
    energy = jnp.zeros((128, N), F32)

    def put(slot, x, even, odd):
        for low, value in ((0, even + odd), (1, even - odd)):
            sent[pl.ds(slot * 8 + low * 4 + x, 128, stride=ROWS_OUT), :] = value

    def piece(f, pair):
        rows = []
        for x in (2 * pair, 2 * pair + 1):
            for part in range(2):
                rows.append(
                    jnp.concatenate(
                        [state[f * 2 + part, pl.ds(h * 4 + x, 64, stride=8), :] for h in range(2)],
                        axis=1,
                    )
                )
        return jnp.concatenate(rows, axis=0)

    for f in order:
        if f == 1:
            for key in ("high0", "low0", "high1", "low1", "state1", "state0"):
                copies[key].wait()
        if f == 2:
            copies["state2"].wait()
            copies["state3"].wait()
        derived = {0: 4, 2: 5}.get(f)
        count = 512 if derived else 256
        share = 0.5 / BRUNT_SQUARED if f == 3 else 0.5
        for pair in range(2):
            value = piece(f, pair)
            square = share * (value * value)
            energy = energy + (square[:128] + square[128:])
            if f == 3:
                moved = value * piece(2, pair)
                flux = flux + (moved[:128] + moved[128:])
            made = product((w_high[:count], w_low[:count]), split(value), ((1,), (1,)))
            for k in range(2):
                x = pair * 2 + k
                cols = slice(k * 128, (k + 1) * 128)
                even, odd = made[0:128, cols], made[128:256, cols]
                put(f, x, even, jnp.where(top, odd, sign * pltpu.roll(odd, 64, 1)))
                if derived:
                    even, odd = made[256:384, cols], made[384:512, cols]
                    even = sign * pltpu.roll(even, 64, 1)
                    put(derived, x, even, jnp.where(top, sign * pltpu.roll(odd, 64, 1), -odd))

    quarter = lanes((1, 128)) // 32
    total = jnp.zeros((1, 128), F32)
    for k, value in enumerate((flux, energy)):
        for which in range(2):
            low = which * GMODES
            part = jnp.sum(value[low : low + 32] + value[64 + low : 96 + low], axis=0, keepdims=True)
            part = part[:, :128] + part[:, 128:]
            part = part + pltpu.roll(part, 64, 1)
            part = part + pltpu.roll(part, 32, 1)
            total = jnp.where(quarter == 2 * k + which, part, total)
    sent[pl.ds(8 * FIELDS_OUT, 128, stride=ROWS_OUT), :] = jnp.broadcast_to(total, (128, 128))


def grid_kernel(
    came,
    groups,
    zt_high,
    zt_low,
    xi_high,
    xi_low,
    xf_high,
    xf_low,
    sent,
    totals,
    wz_high,
    wz_low,
    rows_z,
    planes,
    lines,
):
    picked = slot_rows(groups[...], lax.broadcasted_iota(jnp.int32, (N, N), 0)).astype(BF16)
    for table, out in ((zt_high, wz_high), (zt_low, wz_low)):
        out[...] = jnp.dot(picked, table[...], preferred_element_type=F32).astype(BF16)
    kz = lax.dot_general(
        signed_row((8, N)).astype(F32).astype(BF16),
        picked,
        (((1,), (1,)), ((), ())),
        preferred_element_type=F32,
    )
    kz = kz[0:1, :] * WAVE
    kx = (lax.broadcasted_iota(jnp.int32, (N, 1), 0) % 128).astype(F32) * WAVE
    weights = (wz_high[...], wz_low[...])

    def separate(first, second):
        low = lanes(first.shape) < 64
        return (
            jnp.where(low, first, pltpu.roll(second, 64, 1)),
            jnp.where(low, pltpu.roll(first, 64, 1), second),
        )

    upper = lax.broadcasted_iota(jnp.int32, (16, 8, 128), 1) < 4

    def field(f):
        pieces = []
        for g in range(4):
            lows = [(g * 32 + k) * ROWS_OUT + f * 8 for k in range(32)]
            even = jnp.stack([came[low : low + 8, :] for low in lows[0::2]])
            odd = jnp.stack([came[low : low + 8, :] for low in lows[1::2]])
            first = jnp.where(upper, even, pltpu.roll(odd, 4, 1))
            second = jnp.where(upper, pltpu.roll(even, 4, 1), odd)
            pieces.append(
                jnp.concatenate([first.reshape(128, 128), second.reshape(128, 128)], axis=0)
            )
        near, far = separate(pieces[0], pieces[1]), separate(pieces[2], pieces[3])
        return tuple(jnp.concatenate([near[k], far[k]], axis=1) for k in range(2))

    start = lanes((N, HALF)) == 0

    def vertical(value, slot):
        made = product(split(jnp.concatenate(value, axis=0)), weights, ((1,), (0,)))
        even = (made[:N, :HALF], made[N:, :HALF])
        odd = (made[:N, HALF:], made[N:, HALF:])
        turned = (jnp.where(start, odd[0], -odd[1]), jnp.where(start, odd[1], odd[0]))
        for part in range(2):
            for k, both in enumerate((even[part] + turned[part], even[part] - turned[part])):
                for plane in range(2):
                    col = plane * N + k * HALF
                    rows_z[slot, part * 128 : (part + 1) * 128, col : col + HALF] = both[
                        plane * 128 : (plane + 1) * 128
                    ]

    flow_x = field(0)
    vertical(flow_x, 0)
    flow_z = field(2)
    vertical(flow_z, 2)
    vertical(
        (kx * flow_z[1] - kz * flow_x[1], kz * flow_x[0] - kx * flow_z[0]),
        5,
    )
    flow_y = field(1)
    vertical(flow_y, 1)
    slope = field(5)
    vertical((slope[0] + kz * flow_y[1], slope[1] - kz * flow_y[0]), 4)
    slope = field(4)
    vertical((-(kx * flow_y[1]) - slope[0], kx * flow_y[0] - slope[1]), 6)
    vertical(field(3), 3)

    x_inverse = (xi_high[...], xi_low[...])
    for slot in range(7):
        planes[slot] = product(x_inverse, split(rows_z[slot]), ((1,), (0,)))

    x_forward = (xf_high[...], xf_low[...])
    start_kept = lanes((KEPT_COLS, HALF)) == 0

    def horizontal(value, slot):
        pieces = []
        for plane in range(2):
            near = value[:, plane * N : plane * N + HALF]
            far = value[:, plane * N + HALF : (plane + 1) * N]
            pieces += [near + far, near - far]
        made = product(x_forward, split(jnp.concatenate(pieces, axis=1)), ((1,), (0,)))
        for plane in range(2):
            col = plane * N
            plus = made[:, col : col + HALF]
            odd_real = made[:KEPT_COLS, col + HALF : col + N]
            odd_imag = made[KEPT_COLS:, col + HALF : col + N]
            real, imag = plane * KEPT_COLS, (2 + plane) * KEPT_COLS
            lines[slot, real : real + KEPT_COLS, :HALF] = plus[:KEPT_COLS]
            lines[slot, imag : imag + KEPT_COLS, :HALF] = plus[KEPT_COLS:]
            lines[slot, real : real + KEPT_COLS, HALF:] = jnp.where(start_kept, odd_real, odd_imag)
            lines[slot, imag : imag + KEPT_COLS, HALF:] = jnp.where(
                start_kept, odd_imag, -odd_real
            )

    u, v, w, b, ox, oy, oz = range(7)
    horizontal(planes[v] * planes[oz] - planes[w] * planes[oy], 0)
    horizontal(planes[w] * planes[ox] - planes[u] * planes[oz], 1)
    horizontal(planes[u] * planes[oy] - planes[v] * planes[ox], 2)
    horizontal(planes[u] * planes[b], 3)
    horizontal(planes[v] * planes[b], 4)
    horizontal(planes[w] * planes[b], 5)

    row = lax.broadcasted_iota(jnp.int32, (4 * KEPT_COLS, 1), 0)
    kx_kept = (row % KEPT_COLS).astype(F32) * WAVE
    upper_kept = lax.broadcasted_iota(jnp.int32, (11, 8, 128), 1) < 4

    def slots(value):
        return product(split(value), weights, ((1,), (1,)))

    for g in range(4):
        low = (g * 32 + 22) * ROWS_BACK
        sent[low : low + 10 * ROWS_BACK] = jnp.zeros((10 * ROWS_BACK, 128), F32)

    def put(value, f):
        for pair in range(2):
            cols = slice(pair * 128, (pair + 1) * 128)
            both = separate(value[: 2 * KEPT_COLS, cols], value[2 * KEPT_COLS :, cols])
            for k in range(2):
                g = 2 * pair + k
                first = both[k][:KEPT_COLS].reshape(11, 8, 128)
                second = both[k][KEPT_COLS:].reshape(11, 8, 128)
                even = jnp.where(upper_kept, first, pltpu.roll(second, 4, 1))
                odd = jnp.where(upper_kept, pltpu.roll(first, 4, 1), second)
                for j in range(11):
                    low = (g * 32 + 2 * j) * ROWS_BACK + f * 8
                    sent[low : low + 8, :] = even[j]
                    sent[low + ROWS_BACK : low + ROWS_BACK + 8, :] = odd[j]

    for k in range(3):
        put(slots(lines[k]), k)
    put(kx_kept * slots(lines[3]) + kz * slots(lines[5]), 3)
    put(slots(lines[4]), 4)
    source_grp = lax.broadcasted_iota(jnp.int32, (128, 128), 0) // 32
    total = came[pl.ds(8 * FIELDS_OUT, 128, stride=ROWS_OUT), :]
    total = jnp.where(source_grp == lax.axis_index("grp"), total, 0.0)
    totals[...] = jnp.broadcast_to(jnp.sum(total, axis=0, keepdims=True), (8, 128))


BLOCK = 8


def update_kernel(
    came, totals, state, factors, yf_high, yf_low, made_far, left_high, left_low, got, made_state, sems
):
    slab = lax.axis_index(SLAB)
    total = totals[0:1, :]
    quarter = lanes((1, 128)) // 32
    means = [
        jnp.sum(jnp.where(quarter == k, total, 0.0), axis=1, keepdims=True) / (GMODES * KX * N)
        for k in range(4)
    ]
    wave_y = signed_row((1, N)).astype(F32) * WAVE
    start = lanes((64, 128)) == 0
    for x in range(4):
        for f in range(FIELDS_BACK):
            near, far = (
                came[pl.ds(f * 8 + low * 4 + x, 128, stride=ROWS_BACK), :] for low in range(2)
            )
            even, odd = (near + far).T, (near - far).T
            real, imag = odd[:64], odd[64:]
            turned = (jnp.where(start, real, imag), jnp.where(start, imag, -real))
            rows = slice((x * FIELDS_BACK + f) * 128, (x * FIELDS_BACK + f + 1) * 128)
            left_high[rows, :128], left_low[rows, :128] = split(even)
            left_high[rows, 128:], left_low[rows, 128:] = split(jnp.concatenate(turned, axis=0))
        rows = slice(x * FIELDS_BACK * 128, (x + 1) * FIELDS_BACK * 128)
        got[rows] = product(
            (left_high[rows], left_low[rows]), (yf_high[...], yf_low[...]), ((1,), (0,))
        )

    blocks = 64 // BLOCK

    def out_copy(block):
        rows = pl.ds(pl.multiple_of(block * (8 * BLOCK), 8 * BLOCK), 8 * BLOCK)
        return pltpu.make_async_copy(
            made_state.at[:, rows], made_far.at[:, rows], sems.at[block]
        )

    def step_block(block, carry):
        low = pl.multiple_of(block * BLOCK, BLOCK)
        high = block * BLOCK >= GMODES
        flux = jnp.where(high, means[1], means[0])
        energy = jnp.where(high, means[3], means[2])
        wave_z = factors[6, 0, pl.ds(low, BLOCK)]
        power = factors[6, 1, pl.ds(low, BLOCK)]
        grow = 1.0 + TIME_STEP * ((power - flux) / (2.0 * (energy + EPSILON)))
        for x in range(4):
            wave_x = (slab * 4 + x).astype(F32) * WAVE
            main, turn, slow, lift, inverse_sq, step = (
                factors[k, x, pl.ds(low, BLOCK)] for k in range(6)
            )

            def part(f, k):
                return got[pl.ds((x * FIELDS_BACK + f) * 128 + k * 64 + low, BLOCK)]

            for k in range(2):
                source = part(3, 1 - k) + wave_y * part(4, 1 - k)
                flows = [
                    jnp.concatenate(
                        [
                            state[f * 2 + k, pl.ds(low * 8 + h * 4 + x, BLOCK, stride=8), :]
                            for h in range(2)
                        ],
                        axis=1,
                    )
                    for f in range(4)
                ]
                right = [flows[f] * grow + step * part(f, k) for f in range(3)]
                right_b = flows[3] + (step * source if k == 0 else -(step * source))
                new_x = main * right[0] + turn * right[1]
                new_y = main * right[1] - turn * right[0]
                new_z = slow * right[2] + lift * right_b
                new_b = slow * right_b - BRUNT_SQUARED * (lift * right[2])
                inner = (wave_x * new_x + wave_y * new_y + wave_z * new_z) * inverse_sq
                made = (
                    new_x - wave_x * inner,
                    new_y - wave_y * inner,
                    new_z - wave_z * inner,
                    new_b,
                )
                for f in range(4):
                    for h in range(2):
                        rows = pl.ds(low * 8 + h * 4 + x, BLOCK, stride=8)
                        made_state[f * 2 + k, rows, :] = made[f][:, h * 128 : (h + 1) * 128]
        out_copy(block).start()
        return carry

    lax.fori_loop(0, blocks, step_block, 0)
    for block in range(blocks):
        out_copy(block).wait()


VM = pl.BlockSpec(memory_space=pltpu.VMEM)
HBM = pl.BlockSpec(memory_space=pltpu.HBM)


def far(array):
    return pltpu.with_memory_space_constraint(array, pltpu.HBM)


def granted(mebibytes):
    return pltpu.CompilerParams(vmem_limit_bytes=mebibytes << 20)


def shards(state, kz_group, cutoffs, damping, power):
    y_inverse, z_table, x_inverse, x_forward, y_forward = tables()
    groups = kz_group.reshape(1, N)
    rows = state.reshape(4, 2, 64, 4, 2, 128).transpose(0, 1, 2, 4, 3, 5).reshape(8, 512, 128)

    sent, factors = pl.pallas_call(
        send_kernel,
        out_shape=(
            jax.ShapeDtypeStruct((128 * ROWS_OUT, 128), F32),
            jax.ShapeDtypeStruct((7, 4, 64, N), F32),
        ),
        in_specs=[HBM] * 7,
        out_specs=(VM, VM),
        scratch_shapes=[
            pltpu.SMEM((3,), jnp.int32),
            pltpu.SMEM((GROUPS,), F32),
            pltpu.SMEM((GROUPS,), F32),
            pltpu.VMEM((1, N), jnp.int32),
            pltpu.VMEM((8, 512, 128), F32),
            pltpu.VMEM((512, N), BF16),
            pltpu.VMEM((512, N), BF16),
            pltpu.SemaphoreType.DMA((12,)),
        ],
        compiler_params=granted(SEND_MIB),
        name="send",
    )(*(far(a) for a in (cutoffs, damping, power, groups, rows, *y_inverse)))
    came = lax.all_to_all(sent.reshape(128, 1, ROWS_OUT * 128), ALL, 0, 0, tiled=True)

    back, totals = pl.pallas_call(
        grid_kernel,
        out_shape=(
            jax.ShapeDtypeStruct((128 * ROWS_BACK, 128), F32),
            jax.ShapeDtypeStruct((8, 128), F32),
        ),
        in_specs=[VM] * 8,
        out_specs=(VM, VM),
        scratch_shapes=[
            pltpu.VMEM((N, N), BF16),
            pltpu.VMEM((N, N), BF16),
            pltpu.VMEM((7, 256, 512), F32),
            pltpu.VMEM((7, 256, 512), F32),
            pltpu.VMEM((6, 4 * KEPT_COLS, N), F32),
        ],
        compiler_params=granted(GRID_MIB),
        name="grid",
    )(came.reshape(128 * ROWS_OUT, 128), groups, *z_table, *x_inverse, *x_forward)
    came = lax.all_to_all(back.reshape(128, ROWS_BACK, 128), ALL, 0, 0, tiled=True)

    made = pl.pallas_call(
        update_kernel,
        out_shape=jax.ShapeDtypeStruct((8, 512, 128), F32),
        in_specs=[VM] * 6,
        out_specs=HBM,
        scratch_shapes=[
            pltpu.VMEM((20 * 128, N), BF16),
            pltpu.VMEM((20 * 128, N), BF16),
            pltpu.VMEM((20 * 128, N), F32),
            pltpu.VMEM((8, 512, 128), F32),
            pltpu.SemaphoreType.DMA((64 // BLOCK,)),
        ],
        compiler_params=granted(UPDATE_MIB),
        name="update",
    )(came.reshape(128 * ROWS_BACK, 128), totals, rows, factors, *y_forward)
    made = made.reshape(4, 2, 64, 2, 4, 128).transpose(0, 1, 2, 4, 3, 5)
    return made.reshape(4, 2, 64, 4, N)


def solution(mesh):
    finer = Mesh(
        mesh.devices.reshape(mesh.shape["grp"], 4, 4, 2), ("grp", "slab_0", "slab_1", "slab_2")
    )
    return jax.shard_map(
        shards,
        mesh=finer,
        in_specs=(P(None, None, "grp", SLAB, None), P(), P(), P(), P()),
        out_specs=P(None, None, "grp", SLAB, None),
        check_vma=False,
    )
```

```python
import functools
import math

import jax
import jax.numpy as jnp
import numpy as np
from jax import lax
from jax.experimental import pallas as pl
from jax.experimental.pallas import tpu as pltpu
from jax.sharding import Mesh
from jax.sharding import PartitionSpec as P

N = 256
GROUPS = 8
KX = 128
GMODES = 32
KEPT_COLS = 88
SLAB = ("slab_0", "slab_1", "slab_2")
ALL = ("grp",) + SLAB
HALF = N // 2

TWO_PI = 6.283185307179586
WAVE = TWO_PI / N
TIME_STEP = 0.25
CORIOLIS = 1.0
BRUNT_SQUARED = 2.0
EPSILON = 1e-06
SCALE = 1.0 / 4096.0
FIELDS_OUT = 6
FIELDS_BACK = 5
ROWS_OUT = 8 * FIELDS_OUT
ROWS_BACK = 8 * FIELDS_BACK + 1
ROWS_SPREAD = ROWS_OUT + 1

SEND_MIB = 24
GRID_MIB = 40
UPDATE_MIB = 28

F32 = jnp.float32
BF16 = jnp.bfloat16


def halves(table):
    high = table.astype(np.float32).astype(jnp.bfloat16)
    low = (table - high.astype(np.float64)).astype(np.float32).astype(jnp.bfloat16)
    return jnp.asarray(high), jnp.asarray(low)


def angle(rows, cols):
    return 2.0 * np.pi / N * (np.outer(rows, cols) % N).astype(np.float64)


def signed(index):
    return np.where(index < N // 2, index, index - N)


def folded():
    theta = angle(np.arange(HALF), np.arange(N))
    cosine, sine = np.cos(theta), np.sin(theta)
    odd = np.arange(N) % 2
    cosine[0], sine[0] = 1 - odd, odd
    return np.stack([cosine, sine])


def tables():
    points = np.arange(N)
    pair = folded()
    wave = (WAVE * signed(points))[None, None, :]
    y_inverse = np.concatenate([pair, wave * pair]).reshape(4 * HALF, N)
    fold = pair.reshape(N, N)
    theta = angle(points, np.arange(KX))
    weight = np.where(np.arange(KX) == 0, 1.0, 2.0) * SCALE
    x_inverse = np.concatenate([np.cos(theta) * weight, -np.sin(theta) * weight], axis=1)
    theta = theta.T[:KEPT_COLS]
    x_forward = np.concatenate([np.cos(theta), -np.sin(theta)], axis=0) * SCALE
    return [halves(t) for t in (y_inverse, fold.T.copy(), x_inverse, x_forward, fold)]


def split(value):
    high = value.astype(BF16)
    low = (value - high.astype(F32)).astype(BF16)
    return high, low


def product(left, right, dims):
    def one(a, b):
        return lax.dot_general(a, b, (dims, ((), ())), preferred_element_type=F32)

    return one(left[0], right[0]) + (one(left[0], right[1]) + one(left[1], right[0]))


def slot_rows(group_row, slots):
    member = (lax.broadcasted_iota(jnp.int32, (GROUPS, N), 0) == group_row).astype(F32)
    earlier = (
        lax.broadcasted_iota(jnp.int32, (N, N), 0) < lax.broadcasted_iota(jnp.int32, (N, N), 1)
    ).astype(F32)
    count = jnp.dot(member.astype(BF16), earlier.astype(BF16), preferred_element_type=F32)
    first = (GMODES * lax.broadcasted_iota(jnp.int32, (GROUPS, N), 0)).astype(F32)
    place = jnp.sum(member * (first + count), axis=0, keepdims=True).astype(jnp.int32)
    return slots == place


def signed_row(shape):
    index = lax.broadcasted_iota(jnp.int32, shape, len(shape) - 1)
    return jnp.where(index < N // 2, index, index - N)


def lanes(shape):
    return lax.broadcasted_iota(jnp.int32, shape, len(shape) - 1)


def fill_factors(cutoffs, damping_of, power_of, groups, factors):
    grp = lax.axis_index("grp")
    slab = lax.axis_index(SLAB)
    here = slot_rows(groups[...], lax.broadcasted_iota(jnp.int32, (64, N), 0) + grp * 64)
    mode_z = jnp.sum(jnp.where(here, signed_row((64, N)), 0), axis=1, keepdims=True)
    mode_y = signed_row((1, N))
    slot = lax.broadcasted_iota(jnp.int32, (64, 1), 0)
    damping = jnp.where(slot < GMODES, damping_of[grp * 2], damping_of[grp * 2 + 1])
    wave_z = mode_z.astype(F32) * WAVE
    wave_y = mode_y.astype(F32) * WAVE
    kept_zy = (96 * jnp.abs(mode_z) <= cutoffs[2] * N) & (96 * jnp.abs(mode_y) <= cutoffs[1] * N)
    wave_zy = wave_y * wave_y + wave_z * wave_z
    rotation = TIME_STEP * CORIOLIS
    for x in range(4):
        mode_x = slab * 4 + x
        wave_x = mode_x.astype(F32) * WAVE
        kept = kept_zy & (96 * mode_x <= cutoffs[0] * N)
        wave_sq = wave_x * wave_x + wave_zy
        implicit = 1.0 + TIME_STEP * damping * wave_sq
        square = implicit * implicit
        first = 1.0 / (square + rotation * rotation)
        second = 1.0 / (square + TIME_STEP * TIME_STEP * BRUNT_SQUARED)
        factors[0, x] = implicit * first
        factors[1, x] = rotation * first
        factors[2, x] = implicit * second
        factors[3, x] = TIME_STEP * second
        factors[4, x] = 1.0 / jnp.where(wave_sq == 0, 1.0, wave_sq)
        factors[5, x] = jnp.where(kept, TIME_STEP, 0.0)
    factors[6, 0] = jnp.broadcast_to(wave_z, (64, N))
    power = jnp.where(slot < GMODES, power_of[grp * 2], power_of[grp * 2 + 1])
    factors[6, 1] = jnp.broadcast_to(power, (64, N))


def send_kernel(
    cutoffs_far,
    damping_far,
    power_far,
    groups_far,
    state_far,
    w_high_far,
    w_low_far,
    sent,
    sums,
    factors,
    cutoffs,
    damping_of,
    power_of,
    groups,
    state,
    w_high,
    w_low,
    spread,
    sems,
):
    copies = {}

    def fetch(key, source, target, k):
        copies[key] = pltpu.make_async_copy(source, target, sems.at[k])
        copies[key].start()

    small = (
        (groups_far, groups),
        (cutoffs_far, cutoffs),
        (damping_far, damping_of),
        (power_far, power_of),
    )
    for k, (source, target) in enumerate(small):
        fetch(k, source, target, 8 + k)
    order = (1, 0, 2, 3)
    for k, low in enumerate((0, N)):
        rows = pl.ds(low, N)
        if k == 0:
            fetch("high0", w_high_far.at[rows], w_high.at[rows], 0)
            fetch("state1", state_far.at[pl.ds(2, 2)], state.at[pl.ds(2, 2)], 1)
            fetch("low0", w_low_far.at[rows], w_low.at[rows], 2)
        else:
            fetch("high1", w_high_far.at[rows], w_high.at[rows], 3)
            fetch("low1", w_low_far.at[rows], w_low.at[rows], 4)
    for k, f in enumerate(order[1:]):
        rows = pl.ds(2 * f, 2)
        fetch("state" + str(f), state_far.at[rows], state.at[rows], 5 + k)

    for k in range(4):
        copies[k].wait()
    fill_factors(cutoffs, damping_of, power_of, groups, factors)

    sign = jnp.where(lanes((HALF, 128)) < 64, -1.0, 1.0).astype(F32)
    top = lax.broadcasted_iota(jnp.int32, (HALF, 128), 0) == 0
    flux = jnp.zeros((128, N), F32)
    energy = jnp.zeros((128, N), F32)

    def put(slot, x, even, odd):
        for low, value in ((0, even + odd), (1, even - odd)):
            spread[pl.ds(slot * 8 + low * 4 + x, 128, stride=ROWS_SPREAD), :] = value

    def piece(f, pair):
        rows = []
        for x in (2 * pair, 2 * pair + 1):
            for part in range(2):
                rows.append(
                    jnp.concatenate(
                        [state[f * 2 + part, pl.ds(h * 4 + x, 64, stride=8), :] for h in range(2)],
                        axis=1,
                    )
                )
        return jnp.concatenate(rows, axis=0)

    for f in order:
        if f == 1:
            for key in ("high0", "low0", "high1", "low1", "state1", "state0"):
                copies[key].wait()
        if f == 2:
            copies["state2"].wait()
            copies["state3"].wait()
        derived = {0: 4, 2: 5}.get(f)
        count = 512 if derived else 256
        share = 0.5 / BRUNT_SQUARED if f == 3 else 0.5
        for pair in range(2):
            value = piece(f, pair)
            square = share * (value * value)
            energy = energy + (square[:128] + square[128:])
            if f == 3:
                moved = value * piece(2, pair)
                flux = flux + (moved[:128] + moved[128:])
            made = product((w_high[:count], w_low[:count]), split(value), ((1,), (1,)))
            for k in range(2):
                x = pair * 2 + k
                cols = slice(k * 128, (k + 1) * 128)
                even, odd = made[0:128, cols], made[128:256, cols]
                put(f, x, even, jnp.where(top, odd, sign * pltpu.roll(odd, 64, 1)))
                if derived:
                    even, odd = made[256:384, cols], made[384:512, cols]
                    even = sign * pltpu.roll(even, 64, 1)
                    put(derived, x, even, jnp.where(top, sign * pltpu.roll(odd, 64, 1), -odd))
        for slot in (f, derived) if derived else (f,):
            for device in range(128):
                low, far_low = device * ROWS_OUT + slot * 8, device * ROWS_SPREAD + slot * 8
                sent[low : low + 8, :] = spread[far_low : far_low + 8, :]

    quarter = lanes((1, 128)) // 32
    total = jnp.zeros((1, 128), F32)
    for k, value in enumerate((flux, energy)):
        for which in range(2):
            low = which * GMODES
            part = jnp.sum(value[low : low + 32] + value[64 + low : 96 + low], axis=0, keepdims=True)
            part = part[:, :128] + part[:, 128:]
            part = part + pltpu.roll(part, 64, 1)
            part = part + pltpu.roll(part, 32, 1)
            total = jnp.where(quarter == 2 * k + which, part, total)
    sums[...] = jnp.broadcast_to(total, (8, 128))


def grid_kernel(
    came,
    sums,
    groups,
    zt_high,
    zt_low,
    xi_high,
    xi_low,
    xf_high,
    xf_low,
    sent,
    wz_high,
    wz_low,
    rows_z,
    planes,
    lines,
):
    picked = slot_rows(groups[...], lax.broadcasted_iota(jnp.int32, (N, N), 0)).astype(BF16)
    for table, out in ((zt_high, wz_high), (zt_low, wz_low)):
        out[...] = jnp.dot(picked, table[...], preferred_element_type=F32).astype(BF16)
    kz = lax.dot_general(
        signed_row((8, N)).astype(F32).astype(BF16),
        picked,
        (((1,), (1,)), ((), ())),
        preferred_element_type=F32,
    )
    kz = kz[0:1, :] * WAVE
    kx = (lax.broadcasted_iota(jnp.int32, (N, 1), 0) % 128).astype(F32) * WAVE
    weights = (wz_high[...], wz_low[...])

    def separate(first, second):
        low = lanes(first.shape) < 64
        return (
            jnp.where(low, first, pltpu.roll(second, 64, 1)),
            jnp.where(low, pltpu.roll(first, 64, 1), second),
        )

    upper = lax.broadcasted_iota(jnp.int32, (16, 8, 128), 1) < 4

    def field(f):
        pieces = []
        for g in range(4):
            tiles = came[g * 32 : (g + 1) * 32, f * 8 : (f + 1) * 8, :].reshape(16, 2, 8, 128)
            even, odd = tiles[:, 0], tiles[:, 1]
            first = jnp.where(upper, even, pltpu.roll(odd, 4, 1))
            second = jnp.where(upper, pltpu.roll(even, 4, 1), odd)
            pieces.append(
                jnp.concatenate([first.reshape(128, 128), second.reshape(128, 128)], axis=0)
            )
        near, far = separate(pieces[0], pieces[1]), separate(pieces[2], pieces[3])
        return tuple(jnp.concatenate([near[k], far[k]], axis=1) for k in range(2))

    start = lanes((N, HALF)) == 0

    def vertical(value, slot):
        made = product(split(jnp.concatenate(value, axis=0)), weights, ((1,), (0,)))
        even = (made[:N, :HALF], made[N:, :HALF])
        odd = (made[:N, HALF:], made[N:, HALF:])
        turned = (jnp.where(start, odd[0], -odd[1]), jnp.where(start, odd[1], odd[0]))
        for part in range(2):
            for k, both in enumerate((even[part] + turned[part], even[part] - turned[part])):
                for plane in range(2):
                    col = plane * N + k * HALF
                    rows_z[slot, part * 128 : (part + 1) * 128, col : col + HALF] = both[
                        plane * 128 : (plane + 1) * 128
                    ]

    flow_x = field(0)
    vertical(flow_x, 0)
    flow_z = field(2)
    vertical(flow_z, 2)
    vertical(
        (kx * flow_z[1] - kz * flow_x[1], kz * flow_x[0] - kx * flow_z[0]),
        5,
    )
    flow_y = field(1)
    vertical(flow_y, 1)
    slope = field(5)
    vertical((slope[0] + kz * flow_y[1], slope[1] - kz * flow_y[0]), 4)
    slope = field(4)
    vertical((-(kx * flow_y[1]) - slope[0], kx * flow_y[0] - slope[1]), 6)
    vertical(field(3), 3)

    x_inverse = (xi_high[...], xi_low[...])
    for slot in range(7):
        planes[slot] = product(x_inverse, split(rows_z[slot]), ((1,), (0,)))

    x_forward = (xf_high[...], xf_low[...])
    start_kept = lanes((KEPT_COLS, HALF)) == 0

    def horizontal(value, slot):
        pieces = []
        for plane in range(2):
            near = value[:, plane * N : plane * N + HALF]
            far = value[:, plane * N + HALF : (plane + 1) * N]
            pieces += [near + far, near - far]
        made = product(x_forward, split(jnp.concatenate(pieces, axis=1)), ((1,), (0,)))
        for plane in range(2):
            col = plane * N
            plus = made[:, col : col + HALF]
            odd_real = made[:KEPT_COLS, col + HALF : col + N]
            odd_imag = made[KEPT_COLS:, col + HALF : col + N]
            real, imag = plane * KEPT_COLS, (2 + plane) * KEPT_COLS
            lines[slot, real : real + KEPT_COLS, :HALF] = plus[:KEPT_COLS]
            lines[slot, imag : imag + KEPT_COLS, :HALF] = plus[KEPT_COLS:]
            lines[slot, real : real + KEPT_COLS, HALF:] = jnp.where(start_kept, odd_real, odd_imag)
            lines[slot, imag : imag + KEPT_COLS, HALF:] = jnp.where(
                start_kept, odd_imag, -odd_real
            )

    u, v, w, b, ox, oy, oz = range(7)
    horizontal(planes[v] * planes[oz] - planes[w] * planes[oy], 0)
    horizontal(planes[w] * planes[ox] - planes[u] * planes[oz], 1)
    horizontal(planes[u] * planes[oy] - planes[v] * planes[ox], 2)
    horizontal(planes[u] * planes[b], 3)
    horizontal(planes[v] * planes[b], 4)
    horizontal(planes[w] * planes[b], 5)

    row = lax.broadcasted_iota(jnp.int32, (4 * KEPT_COLS, 1), 0)
    kx_kept = (row % KEPT_COLS).astype(F32) * WAVE
    upper_kept = lax.broadcasted_iota(jnp.int32, (11, 8, 128), 1) < 4

    def slots(value):
        return product(split(value), weights, ((1,), (1,)))

    for g in range(4):
        low = (g * 32 + 22) * ROWS_BACK
        sent[low : low + 10 * ROWS_BACK] = jnp.zeros((10 * ROWS_BACK, 128), F32)

    def put(value, f):
        for pair in range(2):
            cols = slice(pair * 128, (pair + 1) * 128)
            both = separate(value[: 2 * KEPT_COLS, cols], value[2 * KEPT_COLS :, cols])
            for k in range(2):
                g = 2 * pair + k
                first = both[k][:KEPT_COLS].reshape(11, 8, 128)
                second = both[k][KEPT_COLS:].reshape(11, 8, 128)
                even = jnp.where(upper_kept, first, pltpu.roll(second, 4, 1))
                odd = jnp.where(upper_kept, pltpu.roll(first, 4, 1), second)
                for j in range(11):
                    low = (g * 32 + 2 * j) * ROWS_BACK + f * 8
                    sent[low : low + 8, :] = even[j]
                    sent[low + ROWS_BACK : low + ROWS_BACK + 8, :] = odd[j]

    for k in range(3):
        put(slots(lines[k]), k)
    put(kx_kept * slots(lines[3]) + kz * slots(lines[5]), 3)
    put(slots(lines[4]), 4)
    sent[pl.ds(8 * FIELDS_BACK, 128, stride=ROWS_BACK), :] = jnp.broadcast_to(
        sums[0:1, :], (128, 128)
    )


BLOCK = 8


def update_kernel(
    came, state, factors, yf_high, yf_low, made_far, left_high, left_low, got, made_state, sems
):
    grp = lax.axis_index("grp")
    slab = lax.axis_index(SLAB)
    source_grp = lax.broadcasted_iota(jnp.int32, (128, 128), 0) // 32
    total = came[pl.ds(8 * FIELDS_BACK, 128, stride=ROWS_BACK), :]
    total = jnp.sum(jnp.where(source_grp == grp, total, 0.0), axis=0, keepdims=True)
    quarter = lanes((1, 128)) // 32
    means = [
        jnp.sum(jnp.where(quarter == k, total, 0.0), axis=1, keepdims=True) / (GMODES * KX * N)
        for k in range(4)
    ]
    wave_y = signed_row((1, N)).astype(F32) * WAVE
    start = lanes((64, 128)) == 0
    for x in range(4):
        for f in range(FIELDS_BACK):
            near, far = (
                came[pl.ds(f * 8 + low * 4 + x, 128, stride=ROWS_BACK), :] for low in range(2)
            )
            even, odd = (near + far).T, (near - far).T
            real, imag = odd[:64], odd[64:]
            turned = (jnp.where(start, real, imag), jnp.where(start, imag, -real))
            rows = slice((x * FIELDS_BACK + f) * 128, (x * FIELDS_BACK + f + 1) * 128)
            left_high[rows, :128], left_low[rows, :128] = split(even)
            left_high[rows, 128:], left_low[rows, 128:] = split(jnp.concatenate(turned, axis=0))
        rows = slice(x * FIELDS_BACK * 128, (x + 1) * FIELDS_BACK * 128)
        got[rows] = product(
            (left_high[rows], left_low[rows]), (yf_high[...], yf_low[...]), ((1,), (0,))
        )

    blocks = 64 // BLOCK

    def out_copy(block):
        rows = pl.ds(pl.multiple_of(block * (8 * BLOCK), 8 * BLOCK), 8 * BLOCK)
        return pltpu.make_async_copy(
            made_state.at[:, rows], made_far.at[:, rows], sems.at[block]
        )

    def step_block(block, carry):
        low = pl.multiple_of(block * BLOCK, BLOCK)
        high = block * BLOCK >= GMODES
        flux = jnp.where(high, means[1], means[0])
        energy = jnp.where(high, means[3], means[2])
        wave_z = factors[6, 0, pl.ds(low, BLOCK)]
        power = factors[6, 1, pl.ds(low, BLOCK)]
        grow = 1.0 + TIME_STEP * ((power - flux) / (2.0 * (energy + EPSILON)))
        for x in range(4):
            wave_x = (slab * 4 + x).astype(F32) * WAVE
            main, turn, slow, lift, inverse_sq, step = (
                factors[k, x, pl.ds(low, BLOCK)] for k in range(6)
            )

            def part(f, k):
                return got[pl.ds((x * FIELDS_BACK + f) * 128 + k * 64 + low, BLOCK)]

            for k in range(2):
                source = part(3, 1 - k) + wave_y * part(4, 1 - k)
                flows = [
                    jnp.concatenate(
                        [
                            state[f * 2 + k, pl.ds(low * 8 + h * 4 + x, BLOCK, stride=8), :]
                            for h in range(2)
                        ],
                        axis=1,
                    )
                    for f in range(4)
                ]
                right = [flows[f] * grow + step * part(f, k) for f in range(3)]
                right_b = flows[3] + (step * source if k == 0 else -(step * source))
                new_x = main * right[0] + turn * right[1]
                new_y = main * right[1] - turn * right[0]
                new_z = slow * right[2] + lift * right_b
                new_b = slow * right_b - BRUNT_SQUARED * (lift * right[2])
                inner = (wave_x * new_x + wave_y * new_y + wave_z * new_z) * inverse_sq
                made = (
                    new_x - wave_x * inner,
                    new_y - wave_y * inner,
                    new_z - wave_z * inner,
                    new_b,
                )
                for f in range(4):
                    for h in range(2):
                        rows = pl.ds(low * 8 + h * 4 + x, BLOCK, stride=8)
                        made_state[f * 2 + k, rows, :] = made[f][:, h * 128 : (h + 1) * 128]
        out_copy(block).start()
        return carry

    lax.fori_loop(0, blocks, step_block, 0)
    for block in range(blocks):
        out_copy(block).wait()


VM = pl.BlockSpec(memory_space=pltpu.VMEM)
HBM = pl.BlockSpec(memory_space=pltpu.HBM)


def far(array):
    return pltpu.with_memory_space_constraint(array, pltpu.HBM)


def granted(mebibytes):
    return pltpu.CompilerParams(vmem_limit_bytes=mebibytes << 20)


def shards(state, kz_group, cutoffs, damping, power):
    y_inverse, z_table, x_inverse, x_forward, y_forward = tables()
    groups = kz_group.reshape(1, N)
    rows = state.reshape(4, 2, 64, 4, 2, 128).transpose(0, 1, 2, 4, 3, 5).reshape(8, 512, 128)

    sent, sums, factors = pl.pallas_call(
        send_kernel,
        out_shape=(
            jax.ShapeDtypeStruct((128 * ROWS_OUT, 128), F32),
            jax.ShapeDtypeStruct((8, 128), F32),
            jax.ShapeDtypeStruct((7, 4, 64, N), F32),
        ),
        in_specs=[HBM] * 7,
        out_specs=(VM, VM, VM),
        scratch_shapes=[
            pltpu.SMEM((3,), jnp.int32),
            pltpu.SMEM((GROUPS,), F32),
            pltpu.SMEM((GROUPS,), F32),
            pltpu.VMEM((1, N), jnp.int32),
            pltpu.VMEM((8, 512, 128), F32),
            pltpu.VMEM((512, N), BF16),
            pltpu.VMEM((512, N), BF16),
            pltpu.VMEM((128 * ROWS_SPREAD, 128), F32),
            pltpu.SemaphoreType.DMA((12,)),
        ],
        compiler_params=granted(SEND_MIB),
        name="send",
    )(*(far(a) for a in (cutoffs, damping, power, groups, rows, *y_inverse)))
    came = lax.all_to_all(sent.reshape(128, ROWS_OUT, 128), ALL, 0, 0, tiled=True)

    back = pl.pallas_call(
        grid_kernel,
        out_shape=jax.ShapeDtypeStruct((128 * ROWS_BACK, 128), F32),
        in_specs=[VM] * 9,
        out_specs=VM,
        scratch_shapes=[
            pltpu.VMEM((N, N), BF16),
            pltpu.VMEM((N, N), BF16),
            pltpu.VMEM((7, 256, 512), F32),
            pltpu.VMEM((7, 256, 512), F32),
            pltpu.VMEM((6, 4 * KEPT_COLS, N), F32),
        ],
        compiler_params=granted(GRID_MIB),
        name="grid",
    )(came, sums, groups, *z_table, *x_inverse, *x_forward)
    came = lax.all_to_all(back.reshape(128, 1, ROWS_BACK * 128), ALL, 0, 0, tiled=True)

    made = pl.pallas_call(
        update_kernel,
        out_shape=jax.ShapeDtypeStruct((8, 512, 128), F32),
        in_specs=[VM] * 5,
        out_specs=HBM,
        scratch_shapes=[
            pltpu.VMEM((20 * 128, N), BF16),
            pltpu.VMEM((20 * 128, N), BF16),
            pltpu.VMEM((20 * 128, N), F32),
            pltpu.VMEM((8, 512, 128), F32),
            pltpu.SemaphoreType.DMA((64 // BLOCK,)),
        ],
        compiler_params=granted(UPDATE_MIB),
        name="update",
    )(came.reshape(128 * ROWS_BACK, 128), rows, factors, *y_forward)
    made = made.reshape(4, 2, 64, 2, 4, 128).transpose(0, 1, 2, 4, 3, 5)
    return made.reshape(4, 2, 64, 4, N)


def solution(mesh):
    finer = Mesh(
        mesh.devices.reshape(mesh.shape["grp"], 4, 4, 2), ("grp", "slab_0", "slab_1", "slab_2")
    )
    return jax.shard_map(
        shards,
        mesh=finer,
        in_specs=(P(None, None, "grp", SLAB, None), P(), P(), P(), P()),
        out_specs=P(None, None, "grp", SLAB, None),
        check_vma=False,
    )
```

```python
import functools
import math

import jax
import jax.numpy as jnp
import numpy as np
from jax import lax
from jax.experimental import pallas as pl
from jax.experimental.pallas import tpu as pltpu
from jax.sharding import Mesh
from jax.sharding import PartitionSpec as P

N = 256
GROUPS = 8
KX = 128
GMODES = 32
KEPT_COLS = 88
SLAB = ("slab_0", "slab_1", "slab_2")
ALL = ("grp",) + SLAB
HALF = N // 2

TWO_PI = 6.283185307179586
WAVE = TWO_PI / N
TIME_STEP = 0.25
CORIOLIS = 1.0
BRUNT_SQUARED = 2.0
EPSILON = 1e-06
SCALE = 1.0 / 4096.0
FIELDS_OUT = 6
FIELDS_BACK = 5
ROWS_OUT = 8 * FIELDS_OUT
ROWS_BACK = 8 * FIELDS_BACK + 1
ROWS_SPREAD = ROWS_OUT + 1

SEND_MIB = 24
GRID_MIB = 40
UPDATE_MIB = 28

F32 = jnp.float32
BF16 = jnp.bfloat16


def halves(table):
    high = table.astype(np.float32).astype(jnp.bfloat16)
    low = (table - high.astype(np.float64)).astype(np.float32).astype(jnp.bfloat16)
    return jnp.asarray(high), jnp.asarray(low)


def angle(rows, cols):
    return 2.0 * np.pi / N * (np.outer(rows, cols) % N).astype(np.float64)


def signed(index):
    return np.where(index < N // 2, index, index - N)


def folded():
    theta = angle(np.arange(HALF), np.arange(N))
    cosine, sine = np.cos(theta), np.sin(theta)
    odd = np.arange(N) % 2
    cosine[0], sine[0] = 1 - odd, odd
    return np.stack([cosine, sine])


def tables():
    points = np.arange(N)
    pair = folded()
    wave = (WAVE * signed(points))[None, None, :]
    y_inverse = np.concatenate([pair, wave * pair]).reshape(4 * HALF, N)
    fold = pair.reshape(N, N)
    theta = angle(points, np.arange(KX))
    weight = np.where(np.arange(KX) == 0, 1.0, 2.0) * SCALE
    x_inverse = np.concatenate([np.cos(theta) * weight, -np.sin(theta) * weight], axis=1)
    theta = theta.T[:KEPT_COLS]
    x_forward = np.concatenate([np.cos(theta), -np.sin(theta)], axis=0) * SCALE
    return [halves(t) for t in (y_inverse, fold.T.copy(), x_inverse, x_forward, fold)]


def split(value):
    high = value.astype(BF16)
    low = (value - high.astype(F32)).astype(BF16)
    return high, low


def product(left, right, dims):
    def one(a, b):
        return lax.dot_general(a, b, (dims, ((), ())), preferred_element_type=F32)

    return one(left[0], right[0]) + (one(left[0], right[1]) + one(left[1], right[0]))


def slot_rows(group_row, slots):
    member = (lax.broadcasted_iota(jnp.int32, (GROUPS, N), 0) == group_row).astype(F32)
    earlier = (
        lax.broadcasted_iota(jnp.int32, (N, N), 0) < lax.broadcasted_iota(jnp.int32, (N, N), 1)
    ).astype(F32)
    count = jnp.dot(member.astype(BF16), earlier.astype(BF16), preferred_element_type=F32)
    first = (GMODES * lax.broadcasted_iota(jnp.int32, (GROUPS, N), 0)).astype(F32)
    place = jnp.sum(member * (first + count), axis=0, keepdims=True).astype(jnp.int32)
    return slots == place


def signed_row(shape):
    index = lax.broadcasted_iota(jnp.int32, shape, len(shape) - 1)
    return jnp.where(index < N // 2, index, index - N)


def lanes(shape):
    return lax.broadcasted_iota(jnp.int32, shape, len(shape) - 1)


def fill_factors(cutoffs, damping_of, power_of, groups, factors):
    grp = lax.axis_index("grp")
    slab = lax.axis_index(SLAB)
    here = slot_rows(groups[...], lax.broadcasted_iota(jnp.int32, (64, N), 0) + grp * 64)
    mode_z = jnp.sum(jnp.where(here, signed_row((64, N)), 0), axis=1, keepdims=True)
    mode_y = signed_row((1, N))
    slot = lax.broadcasted_iota(jnp.int32, (64, 1), 0)
    damping = jnp.where(slot < GMODES, damping_of[grp * 2], damping_of[grp * 2 + 1])
    wave_z = mode_z.astype(F32) * WAVE
    wave_y = mode_y.astype(F32) * WAVE
    kept_zy = (96 * jnp.abs(mode_z) <= cutoffs[2] * N) & (96 * jnp.abs(mode_y) <= cutoffs[1] * N)
    wave_zy = wave_y * wave_y + wave_z * wave_z
    rotation = TIME_STEP * CORIOLIS
    for x in range(4):
        mode_x = slab * 4 + x
        wave_x = mode_x.astype(F32) * WAVE
        kept = kept_zy & (96 * mode_x <= cutoffs[0] * N)
        wave_sq = wave_x * wave_x + wave_zy
        implicit = 1.0 + TIME_STEP * damping * wave_sq
        square = implicit * implicit
        first = 1.0 / (square + rotation * rotation)
        second = 1.0 / (square + TIME_STEP * TIME_STEP * BRUNT_SQUARED)
        factors[0, x] = implicit * first
        factors[1, x] = rotation * first
        factors[2, x] = implicit * second
        factors[3, x] = TIME_STEP * second
        factors[4, x] = 1.0 / jnp.where(wave_sq == 0, 1.0, wave_sq)
        factors[5, x] = jnp.where(kept, TIME_STEP, 0.0)
    factors[6, 0] = jnp.broadcast_to(wave_z, (64, N))
    power = jnp.where(slot < GMODES, power_of[grp * 2], power_of[grp * 2 + 1])
    factors[6, 1] = jnp.broadcast_to(power, (64, N))


def send_kernel(
    cutoffs_far,
    damping_far,
    power_far,
    groups_far,
    state_far,
    w_high_far,
    w_low_far,
    sent,
    sums,
    factors,
    cutoffs,
    damping_of,
    power_of,
    groups,
    state,
    w_high,
    w_low,
    spread,
    sems,
):
    copies = {}

    def fetch(key, source, target, k):
        copies[key] = pltpu.make_async_copy(source, target, sems.at[k])
        copies[key].start()

    small = (
        (groups_far, groups),
        (cutoffs_far, cutoffs),
        (damping_far, damping_of),
        (power_far, power_of),
    )
    for k, (source, target) in enumerate(small):
        fetch(k, source, target, 8 + k)
    order = (1, 0, 2, 3)
    for k, low in enumerate((0, N)):
        rows = pl.ds(low, N)
        if k == 0:
            fetch("high0", w_high_far.at[rows], w_high.at[rows], 0)
            fetch("state1", state_far.at[pl.ds(2, 2)], state.at[pl.ds(2, 2)], 1)
            fetch("low0", w_low_far.at[rows], w_low.at[rows], 2)
        else:
            fetch("high1", w_high_far.at[rows], w_high.at[rows], 3)
            fetch("low1", w_low_far.at[rows], w_low.at[rows], 4)
    for k, f in enumerate(order[1:]):
        rows = pl.ds(2 * f, 2)
        fetch("state" + str(f), state_far.at[rows], state.at[rows], 5 + k)

    for k in range(4):
        copies[k].wait()
    fill_factors(cutoffs, damping_of, power_of, groups, factors)

    sign = jnp.where(lanes((HALF, 128)) < 64, -1.0, 1.0).astype(F32)
    top = lax.broadcasted_iota(jnp.int32, (HALF, 128), 0) == 0
    flux = jnp.zeros((128, N), F32)
    energy = jnp.zeros((128, N), F32)

    def put(slot, x, even, odd):
        for low, value in ((0, even + odd), (1, even - odd)):
            spread[pl.ds(slot * 8 + low * 4 + x, 128, stride=ROWS_SPREAD), :] = value

    def piece(f, pair):
        rows = []
        for x in (2 * pair, 2 * pair + 1):
            for part in range(2):
                rows.append(
                    jnp.concatenate(
                        [state[f * 2 + part, pl.ds(h * 4 + x, 64, stride=8), :] for h in range(2)],
                        axis=1,
                    )
                )
        return jnp.concatenate(rows, axis=0)

    for f in order:
        if f == 1:
            for key in ("high0", "low0", "state1"):
                copies[key].wait()
        if f == 0:
            for key in ("high1", "low1", "state0", "state2", "state3"):
                copies[key].wait()
        derived = {0: 4, 2: 5}.get(f)
        count = 512 if derived else 256
        share = 0.5 / BRUNT_SQUARED if f == 3 else 0.5
        for pair in range(2):
            value = piece(f, pair)
            square = share * (value * value)
            energy = energy + (square[:128] + square[128:])
            if f == 3:
                moved = value * piece(2, pair)
                flux = flux + (moved[:128] + moved[128:])
            made = product((w_high[:count], w_low[:count]), split(value), ((1,), (1,)))
            for k in range(2):
                x = pair * 2 + k
                cols = slice(k * 128, (k + 1) * 128)
                even, odd = made[0:128, cols], made[128:256, cols]
                put(f, x, even, jnp.where(top, odd, sign * pltpu.roll(odd, 64, 1)))
                if derived:
                    even, odd = made[256:384, cols], made[384:512, cols]
                    even = sign * pltpu.roll(even, 64, 1)
                    put(derived, x, even, jnp.where(top, sign * pltpu.roll(odd, 64, 1), -odd))
        for slot in (f, derived) if derived else (f,):
            for device in range(128):
                low, far_low = device * ROWS_OUT + slot * 8, device * ROWS_SPREAD + slot * 8
                sent[low : low + 8, :] = spread[far_low : far_low + 8, :]

    quarter = lanes((1, 128)) // 32
    total = jnp.zeros((1, 128), F32)
    for k, value in enumerate((flux, energy)):
        for which in range(2):
            low = which * GMODES
            part = jnp.sum(value[low : low + 32] + value[64 + low : 96 + low], axis=0, keepdims=True)
            part = part[:, :128] + part[:, 128:]
            part = part + pltpu.roll(part, 64, 1)
            part = part + pltpu.roll(part, 32, 1)
            total = jnp.where(quarter == 2 * k + which, part, total)
    sums[...] = jnp.broadcast_to(total, (8, 128))


def grid_kernel(
    came,
    sums,
    groups,
    zt_high,
    zt_low,
    xi_high,
    xi_low,
    xf_high,
    xf_low,
    sent,
    wz_high,
    wz_low,
    rows_z,
    planes,
    lines,
):
    picked = slot_rows(groups[...], lax.broadcasted_iota(jnp.int32, (N, N), 0)).astype(BF16)
    for table, out in ((zt_high, wz_high), (zt_low, wz_low)):
        out[...] = jnp.dot(picked, table[...], preferred_element_type=F32).astype(BF16)
    kz = lax.dot_general(
        signed_row((8, N)).astype(F32).astype(BF16),
        picked,
        (((1,), (1,)), ((), ())),
        preferred_element_type=F32,
    )
    kz = kz[0:1, :] * WAVE
    kx = (lax.broadcasted_iota(jnp.int32, (N, 1), 0) % 128).astype(F32) * WAVE
    weights = (wz_high[...], wz_low[...])

    def separate(first, second):
        low = lanes(first.shape) < 64
        return (
            jnp.where(low, first, pltpu.roll(second, 64, 1)),
            jnp.where(low, pltpu.roll(first, 64, 1), second),
        )

    upper = lax.broadcasted_iota(jnp.int32, (16, 8, 128), 1) < 4

    def field(f):
        pieces = []
        for g in range(4):
            tiles = came[g * 32 : (g + 1) * 32, f * 8 : (f + 1) * 8, :].reshape(16, 2, 8, 128)
            even, odd = tiles[:, 0], tiles[:, 1]
            first = jnp.where(upper, even, pltpu.roll(odd, 4, 1))
            second = jnp.where(upper, pltpu.roll(even, 4, 1), odd)
            pieces.append(
                jnp.concatenate([first.reshape(128, 128), second.reshape(128, 128)], axis=0)
            )
        near, far = separate(pieces[0], pieces[1]), separate(pieces[2], pieces[3])
        return tuple(jnp.concatenate([near[k], far[k]], axis=1) for k in range(2))

    start = lanes((N, HALF)) == 0

    def vertical(value, slot):
        made = product(split(jnp.concatenate(value, axis=0)), weights, ((1,), (0,)))
        even = (made[:N, :HALF], made[N:, :HALF])
        odd = (made[:N, HALF:], made[N:, HALF:])
        turned = (jnp.where(start, odd[0], -odd[1]), jnp.where(start, odd[1], odd[0]))
        for part in range(2):
            for k, both in enumerate((even[part] + turned[part], even[part] - turned[part])):
                for plane in range(2):
                    col = plane * N + k * HALF
                    rows_z[slot, part * 128 : (part + 1) * 128, col : col + HALF] = both[
                        plane * 128 : (plane + 1) * 128
                    ]

    flow_x = field(0)
    vertical(flow_x, 0)
    flow_z = field(2)
    vertical(flow_z, 2)
    vertical(
        (kx * flow_z[1] - kz * flow_x[1], kz * flow_x[0] - kx * flow_z[0]),
        5,
    )
    flow_y = field(1)
    vertical(flow_y, 1)
    slope = field(5)
    vertical((slope[0] + kz * flow_y[1], slope[1] - kz * flow_y[0]), 4)
    slope = field(4)
    vertical((-(kx * flow_y[1]) - slope[0], kx * flow_y[0] - slope[1]), 6)
    vertical(field(3), 3)

    x_inverse = (xi_high[...], xi_low[...])
    for slot in range(7):
        planes[slot] = product(x_inverse, split(rows_z[slot]), ((1,), (0,)))

    x_forward = (xf_high[...], xf_low[...])
    start_kept = lanes((KEPT_COLS, HALF)) == 0

    def horizontal(value, slot):
        pieces = []
        for plane in range(2):
            near = value[:, plane * N : plane * N + HALF]
            far = value[:, plane * N + HALF : (plane + 1) * N]
            pieces += [near + far, near - far]
        made = product(x_forward, split(jnp.concatenate(pieces, axis=1)), ((1,), (0,)))
        for plane in range(2):
            col = plane * N
            plus = made[:, col : col + HALF]
            odd_real = made[:KEPT_COLS, col + HALF : col + N]
            odd_imag = made[KEPT_COLS:, col + HALF : col + N]
            real, imag = plane * KEPT_COLS, (2 + plane) * KEPT_COLS
            lines[slot, real : real + KEPT_COLS, :HALF] = plus[:KEPT_COLS]
            lines[slot, imag : imag + KEPT_COLS, :HALF] = plus[KEPT_COLS:]
            lines[slot, real : real + KEPT_COLS, HALF:] = jnp.where(start_kept, odd_real, odd_imag)
            lines[slot, imag : imag + KEPT_COLS, HALF:] = jnp.where(
                start_kept, odd_imag, -odd_real
            )

    u, v, w, b, ox, oy, oz = range(7)
    horizontal(planes[v] * planes[oz] - planes[w] * planes[oy], 0)
    horizontal(planes[w] * planes[ox] - planes[u] * planes[oz], 1)
    horizontal(planes[u] * planes[oy] - planes[v] * planes[ox], 2)
    horizontal(planes[u] * planes[b], 3)
    horizontal(planes[v] * planes[b], 4)
    horizontal(planes[w] * planes[b], 5)

    row = lax.broadcasted_iota(jnp.int32, (4 * KEPT_COLS, 1), 0)
    kx_kept = (row % KEPT_COLS).astype(F32) * WAVE
    upper_kept = lax.broadcasted_iota(jnp.int32, (11, 8, 128), 1) < 4

    def slots(value):
        return product(split(value), weights, ((1,), (1,)))

    for g in range(4):
        low = (g * 32 + 22) * ROWS_BACK
        sent[low : low + 10 * ROWS_BACK] = jnp.zeros((10 * ROWS_BACK, 128), F32)

    def put(value, f):
        for pair in range(2):
            cols = slice(pair * 128, (pair + 1) * 128)
            both = separate(value[: 2 * KEPT_COLS, cols], value[2 * KEPT_COLS :, cols])
            for k in range(2):
                g = 2 * pair + k
                first = both[k][:KEPT_COLS].reshape(11, 8, 128)
                second = both[k][KEPT_COLS:].reshape(11, 8, 128)
                even = jnp.where(upper_kept, first, pltpu.roll(second, 4, 1))
                odd = jnp.where(upper_kept, pltpu.roll(first, 4, 1), second)
                for j in range(11):
                    low = (g * 32 + 2 * j) * ROWS_BACK + f * 8
                    sent[low : low + 8, :] = even[j]
                    sent[low + ROWS_BACK : low + ROWS_BACK + 8, :] = odd[j]

    for k in range(3):
        put(slots(lines[k]), k)
    put(kx_kept * slots(lines[3]) + kz * slots(lines[5]), 3)
    put(slots(lines[4]), 4)
    sent[pl.ds(8 * FIELDS_BACK, 128, stride=ROWS_BACK), :] = jnp.broadcast_to(
        sums[0:1, :], (128, 128)
    )


BLOCK = 8


def update_kernel(
    came, state, factors, yf_high, yf_low, made_far, left_high, left_low, got, made_state, sems
):
    grp = lax.axis_index("grp")
    slab = lax.axis_index(SLAB)
    source_grp = lax.broadcasted_iota(jnp.int32, (128, 128), 0) // 32
    total = came[pl.ds(8 * FIELDS_BACK, 128, stride=ROWS_BACK), :]
    total = jnp.sum(jnp.where(source_grp == grp, total, 0.0), axis=0, keepdims=True)
    quarter = lanes((1, 128)) // 32
    means = [
        jnp.sum(jnp.where(quarter == k, total, 0.0), axis=1, keepdims=True) / (GMODES * KX * N)
        for k in range(4)
    ]
    wave_y = signed_row((1, N)).astype(F32) * WAVE
    start = lanes((64, 128)) == 0
    for x in range(4):
        for f in range(FIELDS_BACK):
            near, far = (
                came[pl.ds(f * 8 + low * 4 + x, 128, stride=ROWS_BACK), :] for low in range(2)
            )
            even, odd = (near + far).T, (near - far).T
            real, imag = odd[:64], odd[64:]
            turned = (jnp.where(start, real, imag), jnp.where(start, imag, -real))
            rows = slice((x * FIELDS_BACK + f) * 128, (x * FIELDS_BACK + f + 1) * 128)
            left_high[rows, :128], left_low[rows, :128] = split(even)
            left_high[rows, 128:], left_low[rows, 128:] = split(jnp.concatenate(turned, axis=0))
        rows = slice(x * FIELDS_BACK * 128, (x + 1) * FIELDS_BACK * 128)
        got[rows] = product(
            (left_high[rows], left_low[rows]), (yf_high[...], yf_low[...]), ((1,), (0,))
        )

    blocks = 64 // BLOCK

    def out_copy(block):
        rows = pl.ds(pl.multiple_of(block * (8 * BLOCK), 8 * BLOCK), 8 * BLOCK)
        return pltpu.make_async_copy(
            made_state.at[:, rows], made_far.at[:, rows], sems.at[block]
        )

    def step_block(block, carry):
        low = pl.multiple_of(block * BLOCK, BLOCK)
        high = block * BLOCK >= GMODES
        flux = jnp.where(high, means[1], means[0])
        energy = jnp.where(high, means[3], means[2])
        wave_z = factors[6, 0, pl.ds(low, BLOCK)]
        power = factors[6, 1, pl.ds(low, BLOCK)]
        grow = 1.0 + TIME_STEP * ((power - flux) / (2.0 * (energy + EPSILON)))
        for x in range(4):
            wave_x = (slab * 4 + x).astype(F32) * WAVE
            main, turn, slow, lift, inverse_sq, step = (
                factors[k, x, pl.ds(low, BLOCK)] for k in range(6)
            )

            def part(f, k):
                return got[pl.ds((x * FIELDS_BACK + f) * 128 + k * 64 + low, BLOCK)]

            for k in range(2):
                source = part(3, 1 - k) + wave_y * part(4, 1 - k)
                flows = [
                    jnp.concatenate(
                        [
                            state[f * 2 + k, pl.ds(low * 8 + h * 4 + x, BLOCK, stride=8), :]
                            for h in range(2)
                        ],
                        axis=1,
                    )
                    for f in range(4)
                ]
                right = [flows[f] * grow + step * part(f, k) for f in range(3)]
                right_b = flows[3] + (step * source if k == 0 else -(step * source))
                new_x = main * right[0] + turn * right[1]
                new_y = main * right[1] - turn * right[0]
                new_z = slow * right[2] + lift * right_b
                new_b = slow * right_b - BRUNT_SQUARED * (lift * right[2])
                inner = (wave_x * new_x + wave_y * new_y + wave_z * new_z) * inverse_sq
                made = (
                    new_x - wave_x * inner,
                    new_y - wave_y * inner,
                    new_z - wave_z * inner,
                    new_b,
                )
                for f in range(4):
                    for h in range(2):
                        rows = pl.ds(low * 8 + h * 4 + x, BLOCK, stride=8)
                        made_state[f * 2 + k, rows, :] = made[f][:, h * 128 : (h + 1) * 128]
        out_copy(block).start()
        return carry

    lax.fori_loop(0, blocks, step_block, 0)
    for block in range(blocks):
        out_copy(block).wait()


VM = pl.BlockSpec(memory_space=pltpu.VMEM)
HBM = pl.BlockSpec(memory_space=pltpu.HBM)


def far(array):
    return pltpu.with_memory_space_constraint(array, pltpu.HBM)


def granted(mebibytes):
    return pltpu.CompilerParams(vmem_limit_bytes=mebibytes << 20)


def shards(state, kz_group, cutoffs, damping, power):
    y_inverse, z_table, x_inverse, x_forward, y_forward = tables()
    groups = kz_group.reshape(1, N)
    rows = state.reshape(4, 2, 64, 4, 2, 128).transpose(0, 1, 2, 4, 3, 5).reshape(8, 512, 128)

    sent, sums, factors = pl.pallas_call(
        send_kernel,
        out_shape=(
            jax.ShapeDtypeStruct((128 * ROWS_OUT, 128), F32),
            jax.ShapeDtypeStruct((8, 128), F32),
            jax.ShapeDtypeStruct((7, 4, 64, N), F32),
        ),
        in_specs=[HBM] * 7,
        out_specs=(VM, VM, VM),
        scratch_shapes=[
            pltpu.SMEM((3,), jnp.int32),
            pltpu.SMEM((GROUPS,), F32),
            pltpu.SMEM((GROUPS,), F32),
            pltpu.VMEM((1, N), jnp.int32),
            pltpu.VMEM((8, 512, 128), F32),
            pltpu.VMEM((512, N), BF16),
            pltpu.VMEM((512, N), BF16),
            pltpu.VMEM((128 * ROWS_SPREAD, 128), F32),
            pltpu.SemaphoreType.DMA((12,)),
        ],
        compiler_params=granted(SEND_MIB),
        name="send",
    )(*(far(a) for a in (cutoffs, damping, power, groups, rows, *y_inverse)))
    came = lax.all_to_all(sent.reshape(128, ROWS_OUT, 128), ALL, 0, 0, tiled=True)

    back = pl.pallas_call(
        grid_kernel,
        out_shape=jax.ShapeDtypeStruct((128 * ROWS_BACK, 128), F32),
        in_specs=[VM] * 9,
        out_specs=VM,
        scratch_shapes=[
            pltpu.VMEM((N, N), BF16),
            pltpu.VMEM((N, N), BF16),
            pltpu.VMEM((7, 256, 512), F32),
            pltpu.VMEM((7, 256, 512), F32),
            pltpu.VMEM((6, 4 * KEPT_COLS, N), F32),
        ],
        compiler_params=granted(GRID_MIB),
        name="grid",
    )(came, sums, groups, *z_table, *x_inverse, *x_forward)
    came = lax.all_to_all(back.reshape(128, 1, ROWS_BACK * 128), ALL, 0, 0, tiled=True)

    made = pl.pallas_call(
        update_kernel,
        out_shape=jax.ShapeDtypeStruct((8, 512, 128), F32),
        in_specs=[VM] * 5,
        out_specs=HBM,
        scratch_shapes=[
            pltpu.VMEM((20 * 128, N), BF16),
            pltpu.VMEM((20 * 128, N), BF16),
            pltpu.VMEM((20 * 128, N), F32),
            pltpu.VMEM((8, 512, 128), F32),
            pltpu.SemaphoreType.DMA((64 // BLOCK,)),
        ],
        compiler_params=granted(UPDATE_MIB),
        name="update",
    )(came.reshape(128 * ROWS_BACK, 128), rows, factors, *y_forward)
    made = made.reshape(4, 2, 64, 2, 4, 128).transpose(0, 1, 2, 4, 3, 5)
    return made.reshape(4, 2, 64, 4, N)


def solution(mesh):
    finer = Mesh(
        mesh.devices.reshape(mesh.shape["grp"], 4, 4, 2), ("grp", "slab_0", "slab_1", "slab_2")
    )
    return jax.shard_map(
        shards,
        mesh=finer,
        in_specs=(P(None, None, "grp", SLAB, None), P(), P(), P(), P()),
        out_specs=P(None, None, "grp", SLAB, None),
        check_vma=False,
    )
```
